128 devices in a mesh: row: 16 (over z, x), col: 8 (over y, core).
Axes of the slice: x: 4, y: 4, z: 4, core: 2. Of those that a mesh axis runs over, the one named last changes fastest.
Arguments:
- edge_vec: float32 [3, 1024], P(None, ('row', 'col')), may hold values from -8 to 8
- edge_atoms: int32 [2, 1024], P(None, ('row', 'col')), may hold values from 0 to 95
- block_weight: bfloat16 [144, 16384], replicated, may hold values from -0.5 to 0.5
- base_hamiltonian: bfloat16 [12288, 12288], P('row', 'col'), as said below
- lower_bound: float32 [1], replicated, may hold values from -50 to -40
- upper_bound: float32 [1], replicated, may hold values from 40 to 50
Outputs:
- purified: float32 [12288, 12288], P('row', 'col')
The draws below stay inside these ranges and needn't reach their ends.
Inputs may be any that keep to these rules, and one draw needn't show every extreme that they name: `base_hamiltonian`: symmetric.
All inputs are finite; a program needn't handle non-finite values.
Results may differ from the reference program's by a relative error of at most 0.0031.
Values may be sent and summed in bfloat16 or wider, within the bound.
A program may use at most 192 MiB of HBM per device.

```python
import math
import jax
import jax.numpy as jnp
import numpy as np
from jax import lax

ORB = 128
NR = 16
FEAT = 144
NB = 96
NORB = 12288
EDGES = 1024


def draw_base_hamiltonian(key, part):
    raw = jax.random.normal(key, (NORB, NORB), jnp.float32)
    return ((raw + raw.T) * 0.7071).astype(jnp.bfloat16)


def set_ends(array, stream_key, low, high):
    longest = array.shape.index(max(array.shape))
    spots = []
    for shift in (0, 1):
        where = [jax.random.randint(jax.random.fold_in(stream_key, axis), (), 0, length) for axis, length in enumerate(array.shape)]
        where[longest] = (where[longest] + shift) % array.shape[longest]
        spots.append(tuple(where))
    return array.at[spots[0]].set(low).at[spots[1]].set(high)


def levels(own_key, dims, shards, least, top_value):
    loudness = 1.0
    for axis_at, blocks in shards:
        draws = jax.random.uniform(jax.random.fold_in(jax.random.fold_in(own_key, 6), axis_at), (blocks,), jnp.float32, least / len(shards), top_value / len(shards))
        loudness = loudness * jnp.repeat(jnp.exp(draws), dims[axis_at] // blocks).reshape((-1,) + (1,) * (len(dims) - 1 - axis_at))
    return loudness


def cumulative_ranks(amount, slope):
    portions = [(1 << 20) // math.isqrt(rank ** slope) + 1 for rank in range(1, amount + 1)]
    deviation = 1 + sum(portions) // (1 << 30)
    return np.cumsum(np.array([max(1, weight // deviation) for weight in portions]))


def skewed_ids(key, extent, count, lean):
    table = cumulative_ranks(count, lean)
    ticket = jax.random.randint(jax.random.fold_in(key, 1), extent, 0, int(table[count - 1]))
    rank = jnp.searchsorted(jnp.asarray(table, jnp.int32), ticket, side="right")
    return jax.random.permutation(jax.random.fold_in(key, 2), count)[rank].astype(jnp.int32)


def noise(stream_key, extent, scale, reach, cuts=(), kind=jnp.bfloat16):
    gain = levels(stream_key, extent, cuts, -0.22, 0.18) if cuts else 1.0
    drawn = jax.random.normal(stream_key, extent, jnp.float32) * scale * gain
    return jnp.minimum(jnp.maximum(drawn, -reach), reach).astype(kind)


def setup_inputs(seed: int = 0) -> dict:
    arg_keys = jax.random.split(jax.random.key(seed), 7)
    return {
        "edge_vec": noise(arg_keys[0], (3, EDGES), 2.0, 8.0, ((1, 128),), jnp.float32),
        "edge_atoms": set_ends(skewed_ids(arg_keys[1], (2, EDGES), NB, 1), jax.random.fold_in(arg_keys[1], 3), 0, NB - 1).astype(jnp.int32),
        "block_weight": noise(arg_keys[2], (FEAT, ORB * ORB), FEAT ** -0.5, 0.5),
        "base_hamiltonian": draw_base_hamiltonian(jax.random.fold_in(arg_keys[6], 71), 0),
        "lower_bound": jnp.clip(jax.random.uniform(arg_keys[4], (1,), jnp.float32, -50.0, -40.0), -50.0, -40.0),
        "upper_bound": jnp.clip(jax.random.uniform(arg_keys[5], (1,), jnp.float32, 40.0, 50.0), 40.0, 50.0),
    }


def features(edge_vec):
    squared = lax.optimization_barrier(jnp.sum(edge_vec * edge_vec, axis=0))
    radius = jnp.sqrt(squared + 0.25)
    unit_x = edge_vec[0] / radius
    unit_y = edge_vec[1] / radius
    unit_z = edge_vec[2] / radius
    harmonics = jnp.stack([jnp.ones_like(unit_x), unit_x, unit_y, unit_z, unit_x * unit_y, unit_y * unit_z, unit_z * unit_x, unit_x * unit_x - unit_y * unit_y, 3.0 * unit_z * unit_z - 1.0])
    centers = 1.0 + 0.3 * jnp.arange(NR, dtype=jnp.float32)
    radial = jnp.exp(-jnp.square((radius[None, :] - centers[:, None]) / 0.5))
    return (radial[:, None, :] * harmonics[None, :, :]).reshape(NR * 9, edge_vec.shape[1])

def reference(edge_vec, edge_atoms, block_weight, base_hamiltonian, lower_bound, upper_bound):
    embedding = features(edge_vec)
    position = (edge_atoms[0] * NB + edge_atoms[1]).astype(jnp.int32)
    selector = (jnp.arange(NB * NB, dtype=jnp.int32)[:, None] == position[None, :]).astype(jnp.float32)
    coefficient = lax.dot_general(selector, embedding, (((1,), (1,)), ((), ())), precision=lax.Precision.HIGHEST)
    blocks = jnp.dot(coefficient.astype(jnp.bfloat16), block_weight, preferred_element_type=jnp.float32).reshape(NB, NB, ORB, ORB)
    hamiltonian = (blocks + blocks.transpose(1, 0, 3, 2)).transpose(0, 2, 1, 3).reshape(NORB, NORB)
    hamiltonian = hamiltonian + base_hamiltonian.astype(jnp.float32)
    index_rows = jnp.arange(NORB, dtype=jnp.int32)
    diagonal_mask = index_rows[:, None] == index_rows[None, :]
    shifted = jnp.where(diagonal_mask, upper_bound[0], jnp.float32(0.0)) - hamiltonian
    start_density = (shifted / (upper_bound[0] - lower_bound[0])).astype(jnp.bfloat16)
    density_wide = start_density.astype(jnp.float32)
    return jnp.dot(density_wide, density_wide, precision=lax.Precision.HIGHEST)
```

```python
import jax
import jax.numpy as jnp
from jax import lax
from jax.experimental import pallas as pl
from jax.experimental.pallas import tpu as pltpu
from jax.sharding import PartitionSpec as P

ORB = 128
NR = 16
RB = 6
ROWS = 768
COLS = 1536
K = 3072
NJ = 6
JW = COLS // NJ
HALF = ROWS // 2
QUART = ROWS // 4
MESH = pl.DeviceIdType.MESH


def plan():
    z_period, y_period, y_lead = 12.7, 19.0, 8.0
    unit_us, out_us, lag = 1.6, 4.3, 2.0
    events = []
    for j in range(NJ):
        if j == 0:
            events.append((0.0, "b_own", j))
        events.append((z_period * j + 5.7, "b_relay", j))
        if j + 1 < NJ:
            events.append((z_period * j + 5.8, "b_own", j + 1))
        events.append((z_period * (j + 1) + 2.0, "b_done", j))
    for p in range(4):
        start = y_lead + y_period * p
        if p == 0:
            events.append((start, "a_own", p))
        events.append((start + 8.0, "a_relay", p))
        if p + 1 < 4:
            events.append((start + 8.1, "a_own", p + 1))
        events.append((start + 14.5, "a_fwd", p))
        events.append((start + y_period + 1.5, "a_far", p))
        events.append((start + y_period + 4.0, "a_done", p))
    events.sort(key=lambda e: e[0])
    order = []
    now, link = 0.0, 0.0
    a_ok, b_ok = set(), set()
    arrive = {}
    todo = [(p, j) for j in range(NJ) for p in (0, 2, 1, 3)]
    while todo or events:
        while events and events[0][0] <= now:
            _, name, arg = events.pop(0)
            order.append((name, arg))
            if name == "a_done":
                a_ok.add(arg)
            if name == "b_done":
                b_ok.add(arg)
        best = None
        wake = events[0][0] if events else 1e9
        for p, j in todo:
            if p not in a_ok or j not in b_ok:
                continue
            needs = {0: [], 1: [(0, j)], 2: [], 3: [(1, j), (2, j)]}[p]
            if any(n not in arrive for n in needs):
                continue
            at = max([now] + [arrive[n] for n in needs])
            if at <= now:
                rank = (p == 3, j, {0: 0, 2: 1, 1: 2, 3: 3}[p])
                if best is None or rank < best[0]:
                    best = (rank, (p, j))
            else:
                wake = min(wake, at)
        if best is None:
            now = wake
            continue
        p, j = best[1]
        todo.remove((p, j))
        order.append(("unit", p, j))
        now += unit_us
        if p != 3:
            link = max(link, now) + out_us
            arrive[(p, j)] = link + lag
    return order, now


def square_kernel(
    t_ref, o_ref, a, b, s0, s1, s2, rf, rp, rm, out,
    a2_sem, al_sem, ar_sem, af_sem, sb_sem, bl_sem, br_sem, bf_sem, rf_sem, rp_sem, rm_sem,
    a2_snd, a_snd, ay_snd, sb_snd, b_snd, x_snd, own_sem, o_sem,
):
    row = lax.axis_index("row")
    col = lax.axis_index("col")
    z, x, y, c = row // 4, row % 4, col // 2, col % 2
    mod = lambda v: (v + 4) % 4
    dev = lambda zz, xx, yy, cc: (zz * 4 + xx, yy * 2 + cc)
    zr, zl = dev(mod(z + 1), x, y, c), dev(mod(z - 1), x, y, c)
    yr, yl = dev(z, x, mod(y + 1), c), dev(z, x, mod(y - 1), c)
    xr, xl = dev(z, mod(x + 1), y, c), dev(z, mod(x - 1), y, c)
    sib = dev(z, x, y, 1 - c)

    barrier = pltpu.get_barrier_semaphore()
    partners = [zr, zl, yr, yl, sib] + [
        dev(z, mod(x + d), y, cc) for d in (1, 2, 3) for cc in (0, 1)
    ]
    for partner in partners:
        pl.semaphore_signal(barrier, inc=1, device_id=partner, device_id_type=MESH)
    pl.semaphore_wait(barrier, len(partners))

    pending = []

    def remote(src, dst, snd, rcv, target):
        return pltpu.make_async_remote_copy(
            src_ref=src, dst_ref=dst, send_sem=snd, recv_sem=rcv,
            device_id=target, device_id_type=MESH,
        )

    def push(src, dst, snd, rcv, target):
        copy = remote(src, dst, snd, rcv, target)
        copy.start()
        pending.append((None, copy))

    def arrived(dst, rcv):
        remote(dst, dst, own_sem.at[1], rcv, sib).wait_recv()

    def a2(r):
        kk = mod(x - r)
        active = (kk // 2) == c
        cols = pl.ds(pl.multiple_of((kk % 2) * ROWS, ROWS), ROWS)
        place = pl.ds(pl.multiple_of(y * ROWS, ROWS), ROWS)
        for s in range(2):
            for h in range(2):
                p = {0: 3, 2: 0, 1: 1 + h, 3: 2 - h}[r]
                rows = pl.ds(h * HALF + s * QUART, QUART)
                src = t_ref.at[rows, cols]
                dst = a.at[p, rows, place]
                if r:
                    copy = remote(src, dst, a2_snd.at[r, s, h], a2_sem.at[p, s], dev(z, kk, y, h))
                    cond = active
                    pl.when(cond)(copy.start)
                    pending.append((cond, copy))
                else:
                    copy = remote(src, dst, a2_snd.at[r, s, h], a2_sem.at[p, s], sib)
                    cond = active & (c != h)
                    pl.when(cond)(copy.start)
                    pending.append((cond, copy))
                    local = pltpu.make_async_copy(src, dst, a2_sem.at[p, s])
                    pl.when(active & (c == h))(local.start)

    def a_piece(p, s, yy):
        return a.at[
            p,
            pl.ds(pl.multiple_of(c * HALF + s * QUART, QUART), QUART),
            pl.ds(pl.multiple_of(yy * ROWS, ROWS), ROWS),
        ]

    def a_half(p, yy, cc):
        return a.at[
            p,
            pl.ds(pl.multiple_of(cc * HALF, HALF), HALF),
            pl.ds(pl.multiple_of(yy * ROWS, ROWS), ROWS),
        ]

    def a_own(p):
        arrived(a_piece(p, 0, y), a2_sem.at[p, 0])
        push(a_piece(p, 0, y), a_piece(p, 0, y), ay_snd.at[p, 0], al_sem.at[p, 0], yr)
        arrived(a_piece(p, 1, y), a2_sem.at[p, 1])
        push(a_piece(p, 1, y), a_piece(p, 1, y), ay_snd.at[p, 1], ar_sem.at[p, 1], yl)
        push(a_piece(p, 1, y), a_piece(p, 1, y), ay_snd.at[p, 2], al_sem.at[p, 1], yr)
        push(a_piece(p, 0, y), a_piece(p, 0, y), ay_snd.at[p, 3], ar_sem.at[p, 0], yl)
        push(a_half(p, y, c), a_half(p, y, c), sb_snd.at[p, 0], sb_sem.at[p, 0], sib)

    def a_relay(p):
        left, right = mod(y - 1), mod(y + 1)
        arrived(a_piece(p, 0, left), al_sem.at[p, 0])
        push(a_piece(p, 0, left), a_piece(p, 0, left), ay_snd.at[p, 4], af_sem.at[p, 0], yr)
        arrived(a_piece(p, 1, right), ar_sem.at[p, 1])
        push(a_piece(p, 1, right), a_piece(p, 1, right), ay_snd.at[p, 5], af_sem.at[p, 1], yl)

    def a_fwd(p):
        left, right = mod(y - 1), mod(y + 1)
        arrived(a_piece(p, 1, left), al_sem.at[p, 1])
        push(a_half(p, left, c), a_half(p, left, c), sb_snd.at[p, 1], sb_sem.at[p, 1], sib)
        arrived(a_piece(p, 0, right), ar_sem.at[p, 0])
        push(a_half(p, right, c), a_half(p, right, c), sb_snd.at[p, 2], sb_sem.at[p, 2], sib)

    def a_far(p):
        far = mod(y + 2)
        arrived(a_piece(p, 0, far), af_sem.at[p, 0])
        arrived(a_piece(p, 1, far), af_sem.at[p, 1])
        push(a_half(p, far, c), a_half(p, far, c), sb_snd.at[p, 3], sb_sem.at[p, 3], sib)

    def a_done(p):
        for i, yy in enumerate((y, mod(y - 1), mod(y + 1), mod(y + 2))):
            arrived(a_half(p, yy, 1 - c), sb_sem.at[p, i])

    def b_piece(j, s, zz):
        return b.at[pl.ds(pl.multiple_of(zz * ROWS + s * HALF, HALF), HALF), pl.ds(j * JW, JW)]

    def b_own(j):
        for i, (s, right) in enumerate(((0, True), (1, False), (1, True), (0, False))):
            src = t_ref.at[pl.ds(s * HALF, HALF), pl.ds(j * JW, JW)]
            rcv = bl_sem.at[j, s] if right else br_sem.at[j, s]
            push(src, b_piece(j, s, z), b_snd.at[j, i], rcv, zr if right else zl)

    def b_relay(j):
        left, right = mod(z - 1), mod(z + 1)
        arrived(b_piece(j, 0, left), bl_sem.at[j, 0])
        push(b_piece(j, 0, left), b_piece(j, 0, left), b_snd.at[j, 4], bf_sem.at[j, 0], zr)
        arrived(b_piece(j, 1, right), br_sem.at[j, 1])
        push(b_piece(j, 1, right), b_piece(j, 1, right), b_snd.at[j, 5], bf_sem.at[j, 1], zl)

    own_tile = b.at[pl.ds(pl.multiple_of(z * ROWS, ROWS), ROWS), :]
    own_copy = pltpu.make_async_copy(t_ref, own_tile, own_sem.at[0])

    def b_done(j):
        if j == 0:
            own_copy.wait()
        arrived(b_piece(j, 1, mod(z - 1)), bl_sem.at[j, 1])
        arrived(b_piece(j, 0, mod(z + 1)), br_sem.at[j, 0])
        for s in range(2):
            arrived(b_piece(j, s, mod(z + 2)), bf_sem.at[j, s])

    def block(ref, j, h):
        return ref.at[pl.ds(h * HALF, HALF), pl.ds(j * JW, JW)]

    def unit(p, j):
        cols = pl.ds(j * JW, JW)
        if p == 1:
            for h in range(2):
                arrived(block(rf, j, h), rf_sem.at[j, h])
        if p == 3:
            for h in range(2):
                arrived(block(rp, j, h), rp_sem.at[j, h])
                arrived(block(rm, j, h), rm_sem.at[j, h])

        def half(h, carry):
            rows = pl.ds(pl.multiple_of(h * HALF, HALF), HALF)
            acc = jnp.dot(a[p, rows, :], b[:, cols], preferred_element_type=jnp.float32)
            if p == 0:
                s0[rows, cols] = acc.astype(jnp.bfloat16)
            elif p == 1:
                s1[rows, cols] = (acc + rf[rows, cols].astype(jnp.float32)).astype(jnp.bfloat16)
            elif p == 2:
                s2[rows, cols] = acc.astype(jnp.bfloat16)
            else:
                out[rows, cols] = (
                    acc + rp[rows, cols].astype(jnp.float32) + rm[rows, cols].astype(jnp.float32)
                )
            return carry

        lax.fori_loop(0, 2, half, 0)
        if p == 0:
            push(block(s0, j, 0), block(rf, j, 0), x_snd.at[p, j, 0], rf_sem.at[j, 0], xr)
            push(block(s0, j, 1), block(rf, j, 1), x_snd.at[p, j, 1], rf_sem.at[j, 1], xl)
        elif p == 1:
            push(block(s1, j, 0), block(rp, j, 0), x_snd.at[p, j, 0], rp_sem.at[j, 0], xr)
            push(block(s1, j, 1), block(rm, j, 1), x_snd.at[p, j, 1], rm_sem.at[j, 1], xl)
        elif p == 2:
            push(block(s2, j, 0), block(rm, j, 0), x_snd.at[p, j, 0], rm_sem.at[j, 0], xl)
            push(block(s2, j, 1), block(rp, j, 1), x_snd.at[p, j, 1], rp_sem.at[j, 1], xr)
        else:
            copy = pltpu.make_async_copy(out.at[:, cols], o_ref.at[:, cols], o_sem.at[j])
            copy.start()
            finals.append(copy)

    finals = []
    for r in (2, 1, 3, 0):
        a2(r)
    steps = {
        "a_own": a_own, "a_relay": a_relay, "a_fwd": a_fwd, "a_far": a_far, "a_done": a_done,
        "b_own": b_own, "b_relay": b_relay, "b_done": b_done, "unit": unit,
    }
    own_copy.start()
    for name, *rest in plan()[0]:
        steps[name](*rest)
    for cond, copy in pending:
        if cond is None:
            copy.wait_send()
        else:
            pl.when(cond)(copy.wait_send)
    for copy in finals:
        copy.wait()


def square(tile):
    dma = pltpu.SemaphoreType.DMA
    bf = jnp.bfloat16
    return pl.pallas_call(
        square_kernel,
        out_shape=jax.ShapeDtypeStruct((ROWS, COLS), jnp.float32),
        in_specs=[pl.BlockSpec(memory_space=pltpu.VMEM)],
        out_specs=pl.BlockSpec(memory_space=pl.ANY),
        scratch_shapes=[
            pltpu.VMEM((4, ROWS, K), bf),
            pltpu.VMEM((K, COLS), bf),
            pltpu.VMEM((ROWS, COLS), bf),
            pltpu.VMEM((ROWS, COLS), bf),
            pltpu.VMEM((ROWS, COLS), bf),
            pltpu.VMEM((ROWS, COLS), bf),
            pltpu.VMEM((ROWS, COLS), bf),
            pltpu.VMEM((ROWS, COLS), bf),
            pltpu.VMEM((ROWS, COLS), jnp.float32),
            dma((4, 2)), dma((4, 2)), dma((4, 2)), dma((4, 2)), dma((4, 4)),
            dma((NJ, 2)), dma((NJ, 2)), dma((NJ, 2)), dma((NJ, 2)), dma((NJ, 2)), dma((NJ, 2)),
            dma((4, 2, 2)), dma((1,)), dma((4, 6)), dma((4, 4)), dma((NJ, 6)), dma((3, NJ, 2)),
            dma((2,)), dma((NJ,)),
        ],
        compiler_params=pltpu.CompilerParams(
            collective_id=0, has_side_effects=True, vmem_limit_bytes=60 * 2**20
        ),
        name="square",
    )(tile)


def features(edge_vec):
    squared = jnp.sum(edge_vec * edge_vec, axis=0)
    radius = jnp.sqrt(squared + 0.25)
    unit_x = edge_vec[0] / radius
    unit_y = edge_vec[1] / radius
    unit_z = edge_vec[2] / radius
    harmonics = jnp.stack(
        [
            jnp.ones_like(unit_x),
            unit_x,
            unit_y,
            unit_z,
            unit_x * unit_y,
            unit_y * unit_z,
            unit_z * unit_x,
            unit_x * unit_x - unit_y * unit_y,
            3.0 * unit_z * unit_z - 1.0,
        ]
    )
    centers = 1.0 + 0.3 * jnp.arange(NR, dtype=jnp.float32)
    radial = jnp.exp(-jnp.square((radius[None, :] - centers[:, None]) / 0.5))
    return (radial[:, None, :] * harmonics[None, :, :]).reshape(NR * 9, edge_vec.shape[1])


def shards(edge_vec, edge_atoms, block_weight, base_hamiltonian, lower_bound, upper_bound):
    atoms_float = edge_atoms.astype(jnp.float32)
    packed = jnp.concatenate([features(edge_vec), atoms_float], axis=0)
    gathered = lax.all_gather(packed, ("row", "col"), axis=1, tiled=True)
    embedding = gathered[:-2]
    atom_pairs = gathered[-2:].astype(jnp.int32)
    first_atom = atom_pairs[0]
    second_atom = atom_pairs[1]
    atoms_total = RB * lax.axis_size("row")
    col_blocks = atoms_total // lax.axis_size("col")
    row_index = lax.axis_index("row")
    col_index = lax.axis_index("col")
    row_atoms = row_index * RB + jnp.arange(RB, dtype=jnp.int32)
    col_atoms = col_index * col_blocks + jnp.arange(col_blocks, dtype=jnp.int32)
    direct = (
        (
            (first_atom[None, None, :] == row_atoms[:, None, None])
            & (second_atom[None, None, :] == col_atoms[None, :, None])
        )
        .astype(jnp.float32)
        .reshape(RB * col_blocks, -1)
    )
    mirror = (
        (
            (first_atom[None, None, :] == col_atoms[None, :, None])
            & (second_atom[None, None, :] == row_atoms[:, None, None])
        )
        .astype(jnp.float32)
        .reshape(RB * col_blocks, -1)
    )
    contract = (((1,), (1,)), ((), ()))
    coefficient = lax.dot_general(
        direct, embedding, contract, precision=lax.Precision.HIGHEST
    ).astype(jnp.bfloat16)
    coefficient_back = lax.dot_general(
        mirror, embedding, contract, precision=lax.Precision.HIGHEST
    ).astype(jnp.bfloat16)
    blocks = jnp.dot(coefficient, block_weight, preferred_element_type=jnp.float32).reshape(
        RB, col_blocks, ORB, ORB
    )
    blocks_back = jnp.dot(
        coefficient_back, block_weight, preferred_element_type=jnp.float32
    ).reshape(RB, col_blocks, ORB, ORB)
    tile_rows = RB * ORB
    tile_cols = col_blocks * ORB
    hamiltonian = (
        (blocks + blocks_back.transpose(0, 1, 3, 2))
        .transpose(0, 2, 1, 3)
        .reshape(tile_rows, tile_cols)
    )
    hamiltonian = hamiltonian + base_hamiltonian.astype(jnp.float32)
    global_rows = row_index * tile_rows + jnp.arange(tile_rows, dtype=jnp.int32)
    global_cols = col_index * tile_cols + jnp.arange(tile_cols, dtype=jnp.int32)
    diagonal_mask = global_rows[:, None] == global_cols[None, :]
    shifted = jnp.where(diagonal_mask, upper_bound[0], jnp.float32(0.0)) - hamiltonian
    start_density = (shifted / (upper_bound[0] - lower_bound[0])).astype(jnp.bfloat16)
    return square(start_density)


def solution(mesh):
    return jax.shard_map(
        shards,
        mesh=mesh,
        in_specs=(P(None, ("row", "col")), P(None, ("row", "col")), P(), P("row", "col"), P(), P()),
        out_specs=P("row", "col"),
        check_vma=False,
    )
```

```python
import jax
import jax.numpy as jnp
from jax import lax
from jax.experimental import pallas as pl
from jax.experimental.pallas import tpu as pltpu
from jax.sharding import PartitionSpec as P

ORB = 128
NR = 16
RB = 6
CB = 12
NB = 96
FEAT = 144
EDGES = 1024
PAIRS = RB * CB
ROWS = 768
COLS = 1536
K = 3072
NJ = 6
JW = COLS // NJ
HALF = ROWS // 2
QUART = ROWS // 4
MESH = pl.DeviceIdType.MESH


def plan():
    z_period, y_period, y_lead = 12.7, 19.0, 8.0
    unit_us, out_us, lag = 1.6, 4.3, 2.0
    events = []
    for j in range(NJ):
        if j == 0:
            events.append((0.0, "b_own", j))
        events.append((z_period * j + 5.7, "b_relay", j))
        if j + 1 < NJ:
            events.append((z_period * j + 5.8, "b_own", j + 1))
        events.append((z_period * (j + 1) + 2.0, "b_done", j))
    for p in range(4):
        start = y_lead + y_period * p
        if p == 0:
            events.append((start, "a_own", p))
        events.append((start + 8.0, "a_relay", p))
        if p + 1 < 4:
            events.append((start + 8.1, "a_own", p + 1))
        events.append((start + 14.5, "a_fwd", p))
        events.append((start + y_period + 1.5, "a_far", p))
        events.append((start + y_period + 4.0, "a_done", p))
    events.sort(key=lambda e: e[0])
    order = []
    now, link = 0.0, 0.0
    a_ok, b_ok = set(), set()
    arrive = {}
    todo = [(p, j) for j in range(NJ) for p in (0, 2, 1, 3)]
    while todo or events:
        while events and events[0][0] <= now:
            _, name, arg = events.pop(0)
            order.append((name, arg))
            if name == "a_done":
                a_ok.add(arg)
            if name == "b_done":
                b_ok.add(arg)
        best = None
        wake = events[0][0] if events else 1e9
        for p, j in todo:
            if p not in a_ok or j not in b_ok:
                continue
            needs = {0: [], 1: [(0, j)], 2: [], 3: [(1, j), (2, j)]}[p]
            if any(n not in arrive for n in needs):
                continue
            at = max([now] + [arrive[n] for n in needs])
            if at <= now:
                rank = (p == 3, j, {0: 0, 2: 1, 1: 2, 3: 3}[p])
                if best is None or rank < best[0]:
                    best = (rank, (p, j))
            else:
                wake = min(wake, at)
        if best is None:
            now = wake
            continue
        p, j = best[1]
        todo.remove((p, j))
        order.append(("unit", p, j))
        now += unit_us
        if p != 3:
            link = max(link, now) + out_us
            arrive[(p, j)] = link + lag
    return order, now


def square_kernel(
    t_ref, o_ref, a, b, s0, s1, s2, rf, rp, rm, out,
    a2_sem, al_sem, ar_sem, af_sem, sb_sem, bl_sem, br_sem, bf_sem, rf_sem, rp_sem, rm_sem,
    a2_snd, a_snd, ay_snd, sb_snd, b_snd, x_snd, own_sem, o_sem,
):
    row = lax.axis_index("row")
    col = lax.axis_index("col")
    z, x, y, c = row // 4, row % 4, col // 2, col % 2
    mod = lambda v: (v + 4) % 4
    dev = lambda zz, xx, yy, cc: (zz * 4 + xx, yy * 2 + cc)
    zr, zl = dev(mod(z + 1), x, y, c), dev(mod(z - 1), x, y, c)
    yr, yl = dev(z, x, mod(y + 1), c), dev(z, x, mod(y - 1), c)
    xr, xl = dev(z, mod(x + 1), y, c), dev(z, mod(x - 1), y, c)
    sib = dev(z, x, y, 1 - c)

    barrier = pltpu.get_barrier_semaphore()
    partners = [zr, zl, yr, yl, sib] + [
        dev(z, mod(x + d), y, cc) for d in (1, 2, 3) for cc in (0, 1)
    ]
    for partner in partners:
        pl.semaphore_signal(barrier, inc=1, device_id=partner, device_id_type=MESH)
    pl.semaphore_wait(barrier, len(partners))

    pending = []

    def remote(src, dst, snd, rcv, target):
        return pltpu.make_async_remote_copy(
            src_ref=src, dst_ref=dst, send_sem=snd, recv_sem=rcv,
            device_id=target, device_id_type=MESH,
        )

    def push(src, dst, snd, rcv, target):
        copy = remote(src, dst, snd, rcv, target)
        copy.start()
        pending.append((None, copy))

    def arrived(dst, rcv):
        remote(dst, dst, own_sem.at[1], rcv, sib).wait_recv()

    def a2(r):
        kk = mod(x - r)
        active = (kk // 2) == c
        cols = pl.ds(pl.multiple_of((kk % 2) * ROWS, ROWS), ROWS)
        place = pl.ds(pl.multiple_of(y * ROWS, ROWS), ROWS)
        for s in range(2):
            for h in range(2):
                p = {0: 3, 2: 0, 1: 1 + h, 3: 2 - h}[r]
                rows = pl.ds(h * HALF + s * QUART, QUART)
                src = t_ref.at[rows, cols]
                dst = a.at[p, rows, place]
                if r:
                    copy = remote(src, dst, a2_snd.at[r, s, h], a2_sem.at[p, s], dev(z, kk, y, h))
                    cond = active
                    pl.when(cond)(copy.start)
                    pending.append((cond, copy))
                else:
                    copy = remote(src, dst, a2_snd.at[r, s, h], a2_sem.at[p, s], sib)
                    cond = active & (c != h)
                    pl.when(cond)(copy.start)
                    pending.append((cond, copy))
                    local = pltpu.make_async_copy(src, dst, a2_sem.at[p, s])
                    pl.when(active & (c == h))(local.start)

    def a_piece(p, s, yy):
        return a.at[
            p,
            pl.ds(pl.multiple_of(c * HALF + s * QUART, QUART), QUART),
            pl.ds(pl.multiple_of(yy * ROWS, ROWS), ROWS),
        ]

    def a_half(p, yy, cc):
        return a.at[
            p,
            pl.ds(pl.multiple_of(cc * HALF, HALF), HALF),
            pl.ds(pl.multiple_of(yy * ROWS, ROWS), ROWS),
        ]

    def a_own(p):
        arrived(a_piece(p, 0, y), a2_sem.at[p, 0])
        push(a_piece(p, 0, y), a_piece(p, 0, y), ay_snd.at[p, 0], al_sem.at[p, 0], yr)
        arrived(a_piece(p, 1, y), a2_sem.at[p, 1])
        push(a_piece(p, 1, y), a_piece(p, 1, y), ay_snd.at[p, 1], ar_sem.at[p, 1], yl)
        push(a_piece(p, 1, y), a_piece(p, 1, y), ay_snd.at[p, 2], al_sem.at[p, 1], yr)
        push(a_piece(p, 0, y), a_piece(p, 0, y), ay_snd.at[p, 3], ar_sem.at[p, 0], yl)
        push(a_half(p, y, c), a_half(p, y, c), sb_snd.at[p, 0], sb_sem.at[p, 0], sib)

    def a_relay(p):
        left, right = mod(y - 1), mod(y + 1)
        arrived(a_piece(p, 0, left), al_sem.at[p, 0])
        push(a_piece(p, 0, left), a_piece(p, 0, left), ay_snd.at[p, 4], af_sem.at[p, 0], yr)
        arrived(a_piece(p, 1, right), ar_sem.at[p, 1])
        push(a_piece(p, 1, right), a_piece(p, 1, right), ay_snd.at[p, 5], af_sem.at[p, 1], yl)

    def a_fwd(p):
        left, right = mod(y - 1), mod(y + 1)
        arrived(a_piece(p, 1, left), al_sem.at[p, 1])
        push(a_half(p, left, c), a_half(p, left, c), sb_snd.at[p, 1], sb_sem.at[p, 1], sib)
        arrived(a_piece(p, 0, right), ar_sem.at[p, 0])
        push(a_half(p, right, c), a_half(p, right, c), sb_snd.at[p, 2], sb_sem.at[p, 2], sib)

    def a_far(p):
        far = mod(y + 2)
        arrived(a_piece(p, 0, far), af_sem.at[p, 0])
        arrived(a_piece(p, 1, far), af_sem.at[p, 1])
        push(a_half(p, far, c), a_half(p, far, c), sb_snd.at[p, 3], sb_sem.at[p, 3], sib)

    def a_done(p):
        for i, yy in enumerate((y, mod(y - 1), mod(y + 1), mod(y + 2))):
            arrived(a_half(p, yy, 1 - c), sb_sem.at[p, i])

    def b_piece(j, s, zz):
        return b.at[pl.ds(pl.multiple_of(zz * ROWS + s * HALF, HALF), HALF), pl.ds(j * JW, JW)]

    def b_own(j):
        for i, (s, right) in enumerate(((0, True), (1, False), (1, True), (0, False))):
            src = t_ref.at[pl.ds(s * HALF, HALF), pl.ds(j * JW, JW)]
            rcv = bl_sem.at[j, s] if right else br_sem.at[j, s]
            push(src, b_piece(j, s, z), b_snd.at[j, i], rcv, zr if right else zl)

    def b_relay(j):
        left, right = mod(z - 1), mod(z + 1)
        arrived(b_piece(j, 0, left), bl_sem.at[j, 0])
        push(b_piece(j, 0, left), b_piece(j, 0, left), b_snd.at[j, 4], bf_sem.at[j, 0], zr)
        arrived(b_piece(j, 1, right), br_sem.at[j, 1])
        push(b_piece(j, 1, right), b_piece(j, 1, right), b_snd.at[j, 5], bf_sem.at[j, 1], zl)

    own_tile = b.at[pl.ds(pl.multiple_of(z * ROWS, ROWS), ROWS), :]
    own_copy = pltpu.make_async_copy(t_ref, own_tile, own_sem.at[0])

    def b_done(j):
        if j == 0:
            own_copy.wait()
        arrived(b_piece(j, 1, mod(z - 1)), bl_sem.at[j, 1])
        arrived(b_piece(j, 0, mod(z + 1)), br_sem.at[j, 0])
        for s in range(2):
            arrived(b_piece(j, s, mod(z + 2)), bf_sem.at[j, s])

    def block(ref, j, h):
        return ref.at[pl.ds(h * HALF, HALF), pl.ds(j * JW, JW)]

    def unit(p, j):
        cols = pl.ds(j * JW, JW)
        if p == 1:
            for h in range(2):
                arrived(block(rf, j, h), rf_sem.at[j, h])
        if p == 3:
            for h in range(2):
                arrived(block(rp, j, h), rp_sem.at[j, h])
                arrived(block(rm, j, h), rm_sem.at[j, h])

        def half(h, carry):
            rows = pl.ds(pl.multiple_of(h * HALF, HALF), HALF)
            acc = jnp.dot(a[p, rows, :], b[:, cols], preferred_element_type=jnp.float32)
            if p == 0:
                s0[rows, cols] = acc.astype(jnp.bfloat16)
            elif p == 1:
                s1[rows, cols] = (acc + rf[rows, cols].astype(jnp.float32)).astype(jnp.bfloat16)
            elif p == 2:
                s2[rows, cols] = acc.astype(jnp.bfloat16)
            else:
                out[rows, cols] = (
                    acc + rp[rows, cols].astype(jnp.float32) + rm[rows, cols].astype(jnp.float32)
                )
            return carry

        lax.fori_loop(0, 2, half, 0)
        if p == 0:
            push(block(s0, j, 0), block(rf, j, 0), x_snd.at[p, j, 0], rf_sem.at[j, 0], xr)
            push(block(s0, j, 1), block(rf, j, 1), x_snd.at[p, j, 1], rf_sem.at[j, 1], xl)
        elif p == 1:
            push(block(s1, j, 0), block(rp, j, 0), x_snd.at[p, j, 0], rp_sem.at[j, 0], xr)
            push(block(s1, j, 1), block(rm, j, 1), x_snd.at[p, j, 1], rm_sem.at[j, 1], xl)
        elif p == 2:
            push(block(s2, j, 0), block(rm, j, 0), x_snd.at[p, j, 0], rm_sem.at[j, 0], xl)
            push(block(s2, j, 1), block(rp, j, 1), x_snd.at[p, j, 1], rp_sem.at[j, 1], xr)
        else:
            copy = pltpu.make_async_copy(out.at[:, cols], o_ref.at[:, cols], o_sem.at[j])
            copy.start()
            finals.append(copy)

    finals = []
    for r in (2, 1, 3, 0):
        a2(r)
    steps = {
        "a_own": a_own, "a_relay": a_relay, "a_fwd": a_fwd, "a_far": a_far, "a_done": a_done,
        "b_own": b_own, "b_relay": b_relay, "b_done": b_done, "unit": unit,
    }
    own_copy.start()
    for name, *rest in plan()[0]:
        steps[name](*rest)
    for cond, copy in pending:
        if cond is None:
            copy.wait_send()
        else:
            pl.when(cond)(copy.wait_send)
    for copy in finals:
        copy.wait()


def square(tile):
    dma = pltpu.SemaphoreType.DMA
    bf = jnp.bfloat16
    return pl.pallas_call(
        square_kernel,
        out_shape=jax.ShapeDtypeStruct((ROWS, COLS), jnp.float32),
        in_specs=[pl.BlockSpec(memory_space=pltpu.VMEM)],
        out_specs=pl.BlockSpec(memory_space=pl.ANY),
        scratch_shapes=[
            pltpu.VMEM((4, ROWS, K), bf),
            pltpu.VMEM((K, COLS), bf),
            pltpu.VMEM((ROWS, COLS), bf),
            pltpu.VMEM((ROWS, COLS), bf),
            pltpu.VMEM((ROWS, COLS), bf),
            pltpu.VMEM((ROWS, COLS), bf),
            pltpu.VMEM((ROWS, COLS), bf),
            pltpu.VMEM((ROWS, COLS), bf),
            pltpu.VMEM((ROWS, COLS), jnp.float32),
            dma((4, 2)), dma((4, 2)), dma((4, 2)), dma((4, 2)), dma((4, 4)),
            dma((NJ, 2)), dma((NJ, 2)), dma((NJ, 2)), dma((NJ, 2)), dma((NJ, 2)), dma((NJ, 2)),
            dma((4, 2, 2)), dma((1,)), dma((4, 6)), dma((4, 4)), dma((NJ, 6)), dma((3, NJ, 2)),
            dma((2,)), dma((NJ,)),
        ],
        compiler_params=pltpu.CompilerParams(
            collective_id=0, has_side_effects=True, vmem_limit_bytes=60 * 2**20
        ),
        name="square",
    )(tile)


def density_kernel(
    edge_ref, lower_ref, upper_ref, w_hbm, base_hbm, t_ref,
    edges, emb, wide, sel, w, base, direct, mirror,
    w_sem, base_sem, own_sem, snd, rcv,
):
    row = lax.axis_index("row")
    col = lax.axis_index("col")
    w_copy = pltpu.make_async_copy(w_hbm, w, w_sem)
    base_copy = pltpu.make_async_copy(base_hbm, base, base_sem)
    w_copy.start()
    base_copy.start()

    barrier = pltpu.get_barrier_semaphore()
    for d in range(1, 8):
        pl.semaphore_signal(
            barrier, inc=1, device_id=(row, (col + d) % 8), device_id_type=MESH
        )
    for d in range(1, 16):
        pl.semaphore_signal(
            barrier, inc=1, device_id=((row + d) % 16, col), device_id_type=MESH
        )
    pl.semaphore_wait(barrier, 22)

    mine = row * 8 + col
    own = pltpu.make_async_copy(edge_ref, edges.at[pl.ds(mine, 1), :], own_sem)
    own.start()
    copies = []
    for d in range(1, 8):
        copy = pltpu.make_async_remote_copy(
            src_ref=edge_ref, dst_ref=edges.at[pl.ds(mine, 1), :],
            send_sem=snd.at[d], recv_sem=rcv.at[d],
            device_id=(row, (col + d) % 8), device_id_type=MESH,
        )
        copy.start()
        copies.append(copy)
    own.wait()
    for d in range(1, 8):
        src = row * 8 + (col + 8 - d) % 8
        pltpu.make_async_remote_copy(
            src_ref=edge_ref, dst_ref=edges.at[pl.ds(src, 1), :],
            send_sem=snd.at[d], recv_sem=rcv.at[d],
            device_id=(row, (col + d) % 8), device_id_type=MESH,
        ).wait_recv()

    def group(r):
        return edges.at[pl.ds(pl.multiple_of(r * 8, 8), 8), :]

    for d in range(1, 16):
        copy = pltpu.make_async_remote_copy(
            src_ref=group(row), dst_ref=group(row),
            send_sem=snd.at[7 + d], recv_sem=rcv.at[7 + d],
            device_id=((row + d) % 16, col), device_id_type=MESH,
        )
        copy.start()
        copies.append(copy)
    for d in range(1, 16):
        src = (row + 16 - d) % 16
        pltpu.make_async_remote_copy(
            src_ref=group(src), dst_ref=group(src),
            send_sem=snd.at[7 + d], recv_sem=rcv.at[7 + d],
            device_id=((row + d) % 16, col), device_id_type=MESH,
        ).wait_recv()
    for copy in copies:
        copy.wait_send()

    fields = edges[...].T
    vx, vy, vz = fields[0:8], fields[8:16], fields[16:24]
    first, second = fields[24:32], fields[32:40]
    radius = jnp.sqrt(vx * vx + vy * vy + vz * vz + 0.25)
    ux, uy, uz = vx / radius, vy / radius, vz / radius
    harmonics = [
        None, ux, uy, uz, ux * uy, uy * uz, uz * ux, ux * ux - uy * uy, 3.0 * uz * uz - 1.0
    ]
    for k in range(NR):
        scaled = (radius - (1.0 + 0.3 * k)) / 0.5
        radial = jnp.exp(-(scaled * scaled))
        for m in range(9):
            f = 9 * k + m
            emb[f * 8 : f * 8 + 8, :] = radial if m == 0 else radial * harmonics[m]
    number = lax.broadcasted_iota(jnp.int32, (PAIRS, ORB), 0)
    upper_atom = jnp.zeros((PAIRS, ORB), jnp.int32)
    for n in range(1, RB):
        upper_atom = upper_atom + jnp.where(number >= CB * n, 1, 0)
    pair = (row * RB + upper_atom) * NB + col * CB + number - CB * upper_atom
    pair = pair.astype(jnp.float32)
    forward = first * float(NB) + second
    backward = second * float(NB) + first
    for i in range(8):
        lanes = slice(i * ORB, (i + 1) * ORB)
        sel[0:PAIRS, lanes] = jnp.where(forward[i : i + 1] == pair, 1.0, 0.0)
        sel[PAIRS : 2 * PAIRS, lanes] = jnp.where(backward[i : i + 1] == pair, 1.0, 0.0)
        wide[:, lanes] = emb[pl.ds(i, FEAT, stride=8), :]
    coefficient = lax.dot_general(
        sel[...], wide[...], (((1,), (1,)), ((), ())),
        precision=lax.Precision.HIGHEST, preferred_element_type=jnp.float32,
    ).astype(jnp.bfloat16)

    w_copy.wait()

    def expand(n, carry):
        start = pl.multiple_of(n * 8 * ORB, 8 * ORB)
        part = jnp.dot(
            coefficient, w[:, pl.ds(start, 8 * ORB)], preferred_element_type=jnp.float32
        )
        for s in range(8):
            for g in range(PAIRS // 8):
                place = pl.ds(g * 8 * ORB + n * 8 + s, 8, stride=ORB)
                lanes = slice(s * ORB, (s + 1) * ORB)
                direct[place, :] = part[g * 8 : g * 8 + 8, lanes]
                mirror[place, :] = part[PAIRS + g * 8 : PAIRS + g * 8 + 8, lanes]
        return carry

    lax.fori_loop(0, ORB // 8, expand, 0)
    base_copy.wait()
    upper = upper_ref[0]
    scale = upper - lower_ref[0]
    on_diagonal = lax.broadcasted_iota(jnp.int32, (ORB, ORB), 0) == lax.broadcasted_iota(
        jnp.int32, (ORB, ORB), 1
    )
    for i in range(RB):

        def finish(k, carry):
            at = pl.multiple_of((i * CB + k) * ORB, ORB)
            lanes = pl.ds(pl.multiple_of(k * ORB, ORB), ORB)
            rows = slice(i * ORB, (i + 1) * ORB)
            both = direct[pl.ds(at, ORB), :] + mirror[pl.ds(at, ORB), :].T
            both = both + base[rows, lanes].astype(jnp.float32)
            shift = jnp.where(row * RB + i == col * CB + k, upper, 0.0)
            moved = jnp.where(on_diagonal, shift, 0.0) - both
            t_ref[rows, lanes] = (moved / scale).astype(jnp.bfloat16)
            return carry

        lax.fori_loop(0, CB, finish, 0)


def density(edges, lower, upper, weight, base):
    dma = pltpu.SemaphoreType.DMA
    f32 = jnp.float32
    return pl.pallas_call(
        density_kernel,
        out_shape=jax.ShapeDtypeStruct((ROWS, COLS), jnp.bfloat16),
        in_specs=[
            pl.BlockSpec(memory_space=pltpu.VMEM),
            pl.BlockSpec(memory_space=pltpu.SMEM),
            pl.BlockSpec(memory_space=pltpu.SMEM),
            pl.BlockSpec(memory_space=pl.ANY),
            pl.BlockSpec(memory_space=pl.ANY),
        ],
        out_specs=pl.BlockSpec(memory_space=pltpu.VMEM),
        scratch_shapes=[
            pltpu.VMEM((ORB, ORB), f32),
            pltpu.VMEM((FEAT * 8, ORB), f32),
            pltpu.VMEM((FEAT, EDGES), f32),
            pltpu.VMEM((2 * PAIRS, EDGES), f32),
            pltpu.VMEM((FEAT, ORB * ORB), jnp.bfloat16),
            pltpu.VMEM((ROWS, COLS), jnp.bfloat16),
            pltpu.VMEM((PAIRS * ORB, ORB), f32),
            pltpu.VMEM((PAIRS * ORB, ORB), f32),
            dma, dma, dma, dma((23,)), dma((23,)),
        ],
        compiler_params=pltpu.CompilerParams(
            collective_id=1, has_side_effects=True, vmem_limit_bytes=60 * 2**20
        ),
        name="density",
    )(edges, lower, upper, weight, base)


def shards(edge_vec, edge_atoms, block_weight, base_hamiltonian, lower_bound, upper_bound):
    packed = jnp.concatenate([edge_vec, edge_atoms.astype(jnp.float32)], axis=0)
    packed = jnp.pad(packed.reshape(1, 40), ((0, 0), (0, ORB - 40)))
    return square(density(packed, lower_bound, upper_bound, block_weight, base_hamiltonian))


def solution(mesh):
    return jax.shard_map(
        shards,
        mesh=mesh,
        in_specs=(P(None, ("row", "col")), P(None, ("row", "col")), P(), P("row", "col"), P(), P()),
        out_specs=P("row", "col"),
        check_vma=False,
    )
```

```python
import jax
import jax.numpy as jnp
from jax import lax
from jax.experimental import pallas as pl
from jax.experimental.pallas import tpu as pltpu
from jax.sharding import PartitionSpec as P

ORB = 128
NR = 16
RB = 6
CB = 12
NB = 96
FEAT = 144
EDGES = 1024
PAIRS = RB * CB
ROWS = 768
COLS = 1536
K = 3072
NJ = 6
JW = COLS // NJ
HALF = ROWS // 2
QUART = ROWS // 4
SUB = ROWS // 8
MESH = pl.DeviceIdType.MESH


def plan():
    z_period, y_period = 12.7, 9.5
    unit_us, out_us, lag = 0.85, 2.15, 2.5
    ring = [4, 5, 0, 1, 2, 3, 7]
    events = [(0.0, "a_own", 6), (0.0, "b_own", 0), (6.0, "a_own", ring[0])]
    for j in range(NJ):
        events.append((z_period * j + 5.7, "b_relay", j))
        if j + 1 < NJ:
            events.append((z_period * j + 5.8, "b_own", j + 1))
        events.append((z_period * (j + 1) + 2.5, "b_done", j))
    events.append((17.0, "a_fwd", 6))
    for i, p in enumerate(ring):
        start = 6.3 + y_period * i
        events.append((start + 5.0, "a_relay", p))
        if i + 1 < len(ring):
            events.append((start + 5.1, "a_own", ring[i + 1]))
        else:
            events.append((start + 5.1, "a_relay", 6))
        events.append((start + 8.3, "a_fwd", p))
        events.append((start + y_period + 2.0, "a_far", p))
        events.append((start + y_period + 4.5, "a_done", p))
    last = 6.3 + y_period * len(ring)
    events.append((last + 5.0, "a_far", 6))
    events.append((last + 7.5, "a_done", 6))
    events.sort(key=lambda e: e[0])
    order = []
    now, link = 0.0, 0.0
    a_ok, b_ok = set(), set()
    arrive = {}
    todo = [(p, j) for j in range(NJ) for p in range(8)]
    while todo or events:
        while events and events[0][0] <= now:
            _, name, arg = events.pop(0)
            order.append((name, arg))
            if name == "a_done":
                a_ok.add(arg)
            if name == "b_done":
                b_ok.add(arg)
        best = None
        wake = events[0][0] if events else 1e9
        for p, j in todo:
            if p not in a_ok or j not in b_ok:
                continue
            kind, q = p // 2, p % 2
            needs = {0: [], 1: [(q, j)], 2: [], 3: [(2 + q, j), (4 + q, j)]}[kind]
            if any(n not in arrive for n in needs):
                continue
            at = max([now] + [arrive[n] for n in needs])
            if at <= now:
                rank = (kind == 3, kind == 1, j, p)
                if best is None or rank < best[0]:
                    best = (rank, (p, j))
            else:
                wake = min(wake, at)
        if best is None:
            now = wake
            continue
        p, j = best[1]
        todo.remove((p, j))
        order.append(("unit", p, j))
        now += unit_us
        if p < 6:
            link = max(link, now) + out_us
            arrive[(p, j)] = link + lag
    return order, now


def square_kernel(
    t_ref, o_ref, a, b, s0, s1, s2, rf, rp, rm, out,
    a2_sem, al_sem, ar_sem, af_sem, sb_sem, bl_sem, br_sem, bf_sem, rf_sem, rp_sem, rm_sem,
    a2_snd, ay_snd, sb_snd, b_snd, x_snd, own_sem, o_sem,
):
    row = lax.axis_index("row")
    col = lax.axis_index("col")
    z, x, y, c = row // 4, row % 4, col // 2, col % 2
    mod = lambda v: (v + 4) % 4
    dev = lambda zz, xx, yy, cc: (zz * 4 + xx, yy * 2 + cc)
    zr, zl = dev(mod(z + 1), x, y, c), dev(mod(z - 1), x, y, c)
    yr, yl = dev(z, x, mod(y + 1), c), dev(z, x, mod(y - 1), c)
    xr, xl = dev(z, mod(x + 1), y, c), dev(z, mod(x - 1), y, c)
    sib = dev(z, x, y, 1 - c)

    barrier = pltpu.get_barrier_semaphore()
    partners = [zr, zl, yr, yl, sib] + [
        dev(z, mod(x + d), y, cc) for d in (1, 2, 3) for cc in (0, 1)
    ]
    for partner in partners:
        pl.semaphore_signal(barrier, inc=1, device_id=partner, device_id_type=MESH)
    pl.semaphore_wait(barrier, len(partners))

    pending = []

    def remote(src, dst, snd, rcv, target):
        return pltpu.make_async_remote_copy(
            src_ref=src, dst_ref=dst, send_sem=snd, recv_sem=rcv,
            device_id=target, device_id_type=MESH,
        )

    def push(src, dst, snd, rcv, target):
        copy = remote(src, dst, snd, rcv, target)
        copy.start()
        pending.append((None, copy))

    def arrived(dst, rcv):
        remote(dst, dst, own_sem.at[1], rcv, sib).wait_recv()

    def exchange(r, h, q):
        kk = mod(x - r)
        active = (kk // 2) == c
        cols = pl.ds(pl.multiple_of((kk % 2) * ROWS, ROWS), ROWS)
        place = pl.ds(pl.multiple_of(y * ROWS, ROWS), ROWS)
        p = 2 * {0: 3, 2: 0, 1: 1 + h, 3: 2 - h}[r] + q
        for s in range(2):
            src = t_ref.at[pl.ds(h * HALF + q * QUART + s * SUB, SUB), cols]
            dst = a.at[p, pl.ds(h * QUART + s * SUB, SUB), place]
            snd, rcv = a2_snd.at[r, h, q, s], a2_sem.at[p, s]
            if r:
                copy = remote(src, dst, snd, rcv, dev(z, kk, y, h))
                pl.when(active)(copy.start)
                pending.append((active, copy))
            else:
                copy = remote(src, dst, snd, rcv, sib)
                cond = active & (c != h)
                pl.when(cond)(copy.start)
                pending.append((cond, copy))
                local = pltpu.make_async_copy(src, dst, rcv)
                pl.when(active & (c == h))(local.start)

    def a_piece(p, s, yy):
        return a.at[
            p,
            pl.ds(pl.multiple_of(c * QUART + s * SUB, SUB), SUB),
            pl.ds(pl.multiple_of(yy * ROWS, ROWS), ROWS),
        ]

    def a_half(p, yy, cc):
        return a.at[
            p,
            pl.ds(pl.multiple_of(cc * QUART, QUART), QUART),
            pl.ds(pl.multiple_of(yy * ROWS, ROWS), ROWS),
        ]

    def along(p, s, yy, snd, rcv, target):
        push(a_piece(p, s, yy), a_piece(p, s, yy), ay_snd.at[p, snd], rcv.at[p, s], target)

    def share(p, i, yy):
        push(a_half(p, yy, c), a_half(p, yy, c), sb_snd.at[p, i], sb_sem.at[p, i], sib)

    def a_own(p):
        arrived(a_piece(p, 0, y), a2_sem.at[p, 0])
        along(p, 0, y, 0, al_sem, yr)
        arrived(a_piece(p, 1, y), a2_sem.at[p, 1])
        along(p, 1, y, 1, ar_sem, yl)
        along(p, 1, y, 2, al_sem, yr)
        along(p, 0, y, 3, ar_sem, yl)
        share(p, 0, y)

    def a_relay(p):
        left, right = mod(y - 1), mod(y + 1)
        arrived(a_piece(p, 0, left), al_sem.at[p, 0])
        along(p, 0, left, 4, af_sem, yr)
        arrived(a_piece(p, 1, right), ar_sem.at[p, 1])
        along(p, 1, right, 5, af_sem, yl)

    def a_fwd(p):
        left, right = mod(y - 1), mod(y + 1)
        arrived(a_piece(p, 1, left), al_sem.at[p, 1])
        if p == 6:
            arrived(a_piece(p, 0, left), al_sem.at[p, 0])
        share(p, 1, left)
        arrived(a_piece(p, 0, right), ar_sem.at[p, 0])
        if p == 6:
            arrived(a_piece(p, 1, right), ar_sem.at[p, 1])
        share(p, 2, right)

    def a_late(p):
        left, right = mod(y - 1), mod(y + 1)
        along(p, 0, left, 4, af_sem, yr)
        along(p, 1, right, 5, af_sem, yl)

    def a_far(p):
        far = mod(y + 2)
        arrived(a_piece(p, 0, far), af_sem.at[p, 0])
        arrived(a_piece(p, 1, far), af_sem.at[p, 1])
        share(p, 3, far)

    def a_done(p):
        for i, yy in enumerate((y, mod(y - 1), mod(y + 1), mod(y + 2))):
            arrived(a_half(p, yy, 1 - c), sb_sem.at[p, i])

    def b_piece(j, s, zz):
        return b.at[pl.ds(pl.multiple_of(zz * ROWS + s * HALF, HALF), HALF), pl.ds(j * JW, JW)]

    def b_own(j):
        for i, (s, right) in enumerate(((0, True), (1, False), (1, True), (0, False))):
            src = t_ref.at[pl.ds(s * HALF, HALF), pl.ds(j * JW, JW)]
            rcv = bl_sem.at[j, s] if right else br_sem.at[j, s]
            push(src, b_piece(j, s, z), b_snd.at[j, i], rcv, zr if right else zl)

    def b_relay(j):
        left, right = mod(z - 1), mod(z + 1)
        arrived(b_piece(j, 0, left), bl_sem.at[j, 0])
        push(b_piece(j, 0, left), b_piece(j, 0, left), b_snd.at[j, 4], bf_sem.at[j, 0], zr)
        arrived(b_piece(j, 1, right), br_sem.at[j, 1])
        push(b_piece(j, 1, right), b_piece(j, 1, right), b_snd.at[j, 5], bf_sem.at[j, 1], zl)

    own_tile = b.at[pl.ds(pl.multiple_of(z * ROWS, ROWS), ROWS), :]
    own_copy = pltpu.make_async_copy(t_ref, own_tile, own_sem.at[0])

    def b_done(j):
        if j == 0:
            own_copy.wait()
        arrived(b_piece(j, 1, mod(z - 1)), bl_sem.at[j, 1])
        arrived(b_piece(j, 0, mod(z + 1)), br_sem.at[j, 0])
        for s in range(2):
            arrived(b_piece(j, s, mod(z + 2)), bf_sem.at[j, s])

    def block(ref, q, h, j):
        return ref.at[pl.ds(q * HALF + h * QUART, QUART), pl.ds(j * JW, JW)]

    def unit(p, j):
        kind, q = p // 2, p % 2
        cols = pl.ds(j * JW, JW)
        rows = pl.ds(q * HALF, HALF)
        if kind == 1:
            for h in range(2):
                arrived(block(rf, q, h, j), rf_sem.at[q, h, j])
        if kind == 3:
            for h in range(2):
                arrived(block(rp, q, h, j), rp_sem.at[q, h, j])
                arrived(block(rm, q, h, j), rm_sem.at[q, h, j])
        acc = jnp.dot(a[p], b[:, cols], preferred_element_type=jnp.float32)
        if kind == 0:
            s0[rows, cols] = acc.astype(jnp.bfloat16)
        elif kind == 1:
            s1[rows, cols] = (acc + rf[rows, cols].astype(jnp.float32)).astype(jnp.bfloat16)
        elif kind == 2:
            s2[rows, cols] = acc.astype(jnp.bfloat16)
        else:
            acc = acc + rp[rows, cols].astype(jnp.float32) + rm[rows, cols].astype(jnp.float32)
            out[pl.ds(q * QUART, QUART), cols] = acc[:QUART]
            out[pl.ds(HALF + q * QUART, QUART), cols] = acc[QUART:]
        if kind == 3:
            for h in range(2):
                rows = pl.ds(h * HALF + q * QUART, QUART)
                copy = pltpu.make_async_copy(out.at[rows, cols], o_ref.at[rows, cols], o_sem.at[q, h, j])
                copy.start()
                finals.append(copy)
        else:
            source = (s0, s1, s2)[kind]
            for h in range(2):
                target = xr if (h == 0) == (kind < 2) else xl
                into, sem = (rf, rf_sem) if kind == 0 else (rp, rp_sem) if target is xr else (rm, rm_sem)
                push(
                    block(source, q, h, j), block(into, q, h, j),
                    x_snd.at[p, h, j], sem.at[q, h, j], target,
                )

    finals = []
    for r, hs in ((0, (0, 1)), (1, (1,)), (3, (0,)), (2, (0, 1)), (1, (0,)), (3, (1,))):
        for q in range(2):
            for h in hs:
                exchange(r, h, q)
    steps = {
        "a_own": a_own, "a_relay": a_relay, "a_fwd": a_fwd, "a_far": a_far, "a_done": a_done,
        "b_own": b_own, "b_relay": b_relay, "b_done": b_done, "unit": unit,
    }
    own_copy.start()
    for name, *rest in plan()[0]:
        if name == "a_relay" and rest == [6]:
            a_late(6)
        else:
            steps[name](*rest)
    for cond, copy in pending:
        if cond is None:
            copy.wait_send()
        else:
            pl.when(cond)(copy.wait_send)
    for copy in finals:
        copy.wait()


def square(tile):
    dma = pltpu.SemaphoreType.DMA
    bf = jnp.bfloat16
    return pl.pallas_call(
        square_kernel,
        out_shape=jax.ShapeDtypeStruct((ROWS, COLS), jnp.float32),
        in_specs=[pl.BlockSpec(memory_space=pltpu.VMEM)],
        out_specs=pl.BlockSpec(memory_space=pl.ANY),
        scratch_shapes=[
            pltpu.VMEM((8, HALF, K), bf),
            pltpu.VMEM((K, COLS), bf),
            pltpu.VMEM((ROWS, COLS), bf),
            pltpu.VMEM((ROWS, COLS), bf),
            pltpu.VMEM((ROWS, COLS), bf),
            pltpu.VMEM((ROWS, COLS), bf),
            pltpu.VMEM((ROWS, COLS), bf),
            pltpu.VMEM((ROWS, COLS), bf),
            pltpu.VMEM((ROWS, COLS), jnp.float32),
            dma((8, 2)), dma((8, 2)), dma((8, 2)), dma((8, 2)), dma((8, 4)),
            dma((NJ, 2)), dma((NJ, 2)), dma((NJ, 2)),
            dma((2, 2, NJ)), dma((2, 2, NJ)), dma((2, 2, NJ)),
            dma((4, 2, 2, 2)), dma((8, 6)), dma((8, 4)), dma((NJ, 6)), dma((6, 2, NJ)),
            dma((2,)), dma((2, 2, NJ)),
        ],
        compiler_params=pltpu.CompilerParams(
            collective_id=0, has_side_effects=True, vmem_limit_bytes=60 * 2**20
        ),
        name="square",
    )(tile)


def density_kernel(
    edge_ref, lower_ref, upper_ref, w_hbm, base_hbm, t_ref,
    edges, emb, wide, sel, w, base, direct, mirror,
    w_sem, base_sem, own_sem, snd, rcv,
):
    row = lax.axis_index("row")
    col = lax.axis_index("col")
    w_copy = pltpu.make_async_copy(w_hbm, w, w_sem)
    base_copy = pltpu.make_async_copy(base_hbm, base, base_sem)
    w_copy.start()
    base_copy.start()

    barrier = pltpu.get_barrier_semaphore()
    for d in range(1, 8):
        pl.semaphore_signal(
            barrier, inc=1, device_id=(row, (col + d) % 8), device_id_type=MESH
        )
    for d in range(1, 16):
        pl.semaphore_signal(
            barrier, inc=1, device_id=((row + d) % 16, col), device_id_type=MESH
        )
    pl.semaphore_wait(barrier, 22)

    mine = row * 8 + col
    own = pltpu.make_async_copy(edge_ref, edges.at[pl.ds(mine, 1), :], own_sem)
    own.start()
    copies = []
    for d in range(1, 8):
        copy = pltpu.make_async_remote_copy(
            src_ref=edge_ref, dst_ref=edges.at[pl.ds(mine, 1), :],
            send_sem=snd.at[d], recv_sem=rcv.at[d],
            device_id=(row, (col + d) % 8), device_id_type=MESH,
        )
        copy.start()
        copies.append(copy)
    own.wait()
    for d in range(1, 8):
        src = row * 8 + (col + 8 - d) % 8
        pltpu.make_async_remote_copy(
            src_ref=edge_ref, dst_ref=edges.at[pl.ds(src, 1), :],
            send_sem=snd.at[d], recv_sem=rcv.at[d],
            device_id=(row, (col + d) % 8), device_id_type=MESH,
        ).wait_recv()

    def group(r):
        return edges.at[pl.ds(pl.multiple_of(r * 8, 8), 8), :]

    for d in range(1, 16):
        copy = pltpu.make_async_remote_copy(
            src_ref=group(row), dst_ref=group(row),
            send_sem=snd.at[7 + d], recv_sem=rcv.at[7 + d],
            device_id=((row + d) % 16, col), device_id_type=MESH,
        )
        copy.start()
        copies.append(copy)
    for d in range(1, 16):
        src = (row + 16 - d) % 16
        pltpu.make_async_remote_copy(
            src_ref=group(src), dst_ref=group(src),
            send_sem=snd.at[7 + d], recv_sem=rcv.at[7 + d],
            device_id=((row + d) % 16, col), device_id_type=MESH,
        ).wait_recv()
    for copy in copies:
        copy.wait_send()

    fields = edges[...].T
    vx, vy, vz = fields[0:8], fields[8:16], fields[16:24]
    first, second = fields[24:32], fields[32:40]
    radius = jnp.sqrt(vx * vx + vy * vy + vz * vz + 0.25)
    ux, uy, uz = vx / radius, vy / radius, vz / radius
    harmonics = [
        None, ux, uy, uz, ux * uy, uy * uz, uz * ux, ux * ux - uy * uy, 3.0 * uz * uz - 1.0
    ]
    for k in range(NR):
        scaled = (radius - (1.0 + 0.3 * k)) / 0.5
        radial = jnp.exp(-(scaled * scaled))
        for m in range(9):
            f = 9 * k + m
            emb[f * 8 : f * 8 + 8, :] = radial if m == 0 else radial * harmonics[m]
    number = lax.broadcasted_iota(jnp.int32, (PAIRS, ORB), 0)
    upper_atom = jnp.zeros((PAIRS, ORB), jnp.int32)
    for n in range(1, RB):
        upper_atom = upper_atom + jnp.where(number >= CB * n, 1, 0)
    pair = (row * RB + upper_atom) * NB + col * CB + number - CB * upper_atom
    pair = pair.astype(jnp.float32)
    forward = first * float(NB) + second
    backward = second * float(NB) + first
    for i in range(8):
        lanes = slice(i * ORB, (i + 1) * ORB)
        sel[0:PAIRS, lanes] = jnp.where(forward[i : i + 1] == pair, 1.0, 0.0)
        sel[PAIRS : 2 * PAIRS, lanes] = jnp.where(backward[i : i + 1] == pair, 1.0, 0.0)
        wide[:, lanes] = emb[pl.ds(i, FEAT, stride=8), :]
    coefficient = lax.dot_general(
        sel[...], wide[...], (((1,), (1,)), ((), ())),
        precision=lax.Precision.HIGHEST, preferred_element_type=jnp.float32,
    ).astype(jnp.bfloat16)

    w_copy.wait()

    def expand(n, carry):
        start = pl.multiple_of(n * 8 * ORB, 8 * ORB)
        part = jnp.dot(
            coefficient, w[:, pl.ds(start, 8 * ORB)], preferred_element_type=jnp.float32
        )
        for s in range(8):
            for g in range(PAIRS // 8):
                place = pl.ds(g * 8 * ORB + n * 8 + s, 8, stride=ORB)
                lanes = slice(s * ORB, (s + 1) * ORB)
                direct[place, :] = part[g * 8 : g * 8 + 8, lanes]
                mirror[place, :] = part[PAIRS + g * 8 : PAIRS + g * 8 + 8, lanes]
        return carry

    lax.fori_loop(0, ORB // 8, expand, 0)
    base_copy.wait()
    upper = upper_ref[0]
    scale = upper - lower_ref[0]
    on_diagonal = lax.broadcasted_iota(jnp.int32, (ORB, ORB), 0) == lax.broadcasted_iota(
        jnp.int32, (ORB, ORB), 1
    )
    for i in range(RB):

        def finish(k, carry):
            at = pl.multiple_of((i * CB + k) * ORB, ORB)
            lanes = pl.ds(pl.multiple_of(k * ORB, ORB), ORB)
            rows = slice(i * ORB, (i + 1) * ORB)
            both = direct[pl.ds(at, ORB), :] + mirror[pl.ds(at, ORB), :].T
            both = both + base[rows, lanes].astype(jnp.float32)
            shift = jnp.where(row * RB + i == col * CB + k, upper, 0.0)
            moved = jnp.where(on_diagonal, shift, 0.0) - both
            t_ref[rows, lanes] = (moved / scale).astype(jnp.bfloat16)
            return carry

        lax.fori_loop(0, CB, finish, 0)


def density(edges, lower, upper, weight, base):
    dma = pltpu.SemaphoreType.DMA
    f32 = jnp.float32
    return pl.pallas_call(
        density_kernel,
        out_shape=jax.ShapeDtypeStruct((ROWS, COLS), jnp.bfloat16),
        in_specs=[
            pl.BlockSpec(memory_space=pltpu.VMEM),
            pl.BlockSpec(memory_space=pltpu.SMEM),
            pl.BlockSpec(memory_space=pltpu.SMEM),
            pl.BlockSpec(memory_space=pl.ANY),
            pl.BlockSpec(memory_space=pl.ANY),
        ],
        out_specs=pl.BlockSpec(memory_space=pltpu.VMEM),
        scratch_shapes=[
            pltpu.VMEM((ORB, ORB), f32),
            pltpu.VMEM((FEAT * 8, ORB), f32),
            pltpu.VMEM((FEAT, EDGES), f32),
            pltpu.VMEM((2 * PAIRS, EDGES), f32),
            pltpu.VMEM((FEAT, ORB * ORB), jnp.bfloat16),
            pltpu.VMEM((ROWS, COLS), jnp.bfloat16),
            pltpu.VMEM((PAIRS * ORB, ORB), f32),
            pltpu.VMEM((PAIRS * ORB, ORB), f32),
            dma, dma, dma, dma((23,)), dma((23,)),
        ],
        compiler_params=pltpu.CompilerParams(
            collective_id=1, has_side_effects=True, vmem_limit_bytes=60 * 2**20
        ),
        name="density",
    )(edges, lower, upper, weight, base)


def shards(edge_vec, edge_atoms, block_weight, base_hamiltonian, lower_bound, upper_bound):
    packed = jnp.concatenate([edge_vec, edge_atoms.astype(jnp.float32)], axis=0)
    packed = jnp.pad(packed.reshape(1, 40), ((0, 0), (0, ORB - 40)))
    return square(density(packed, lower_bound, upper_bound, block_weight, base_hamiltonian))


def solution(mesh):
    return jax.shard_map(
        shards,
        mesh=mesh,
        in_specs=(P(None, ("row", "col")), P(None, ("row", "col")), P(), P("row", "col"), P(), P()),
        out_specs=P("row", "col"),
        check_vma=False,
    )
```

```python
import jax
import jax.numpy as jnp
from jax import lax
from jax.experimental import pallas as pl
from jax.experimental.pallas import tpu as pltpu
from jax.sharding import PartitionSpec as P

ORB = 128
NR = 16
RB = 6
CB = 12
NB = 96
FEAT = 144
EDGES = 1024
PAIRS = RB * CB
ROWS = 768
COLS = 1536
K = 3072
NJ = 6
JW = COLS // NJ
HALF = ROWS // 2
QUART = ROWS // 4
SUB = ROWS // 8
MESH = pl.DeviceIdType.MESH


def plan():
    z_period, y_period = 12.7, 9.5
    unit_us, out_us, lag = 0.85, 2.15, 2.5
    ring = [4, 5, 0, 1, 2, 3, 7]
    events = [(0.0, "a_own", 6), (0.0, "b_own", 0), (6.0, "a_own", ring[0])]
    for j in range(NJ):
        events.append((z_period * j + 5.7, "b_relay", j))
        if j + 1 < NJ:
            events.append((z_period * j + 5.8, "b_own", j + 1))
        events.append((z_period * (j + 1) + 2.5, "b_done", j))
    events.append((17.0, "a_fwd", 6))
    for i, p in enumerate(ring):
        start = 6.3 + y_period * i
        events.append((start + 5.0, "a_relay", p))
        if i + 1 < len(ring):
            events.append((start + 5.1, "a_own", ring[i + 1]))
        else:
            events.append((start + 5.1, "a_relay", 6))
        events.append((start + 8.3, "a_fwd", p))
        events.append((start + y_period + 2.0, "a_far", p))
        events.append((start + y_period + 4.5, "a_done", p))
    last = 6.3 + y_period * len(ring)
    events.append((last + 5.0, "a_far", 6))
    events.append((last + 7.5, "a_done", 6))
    events.sort(key=lambda e: e[0])
    order = []
    now, link = 0.0, 0.0
    a_ok, b_ok = set(), set()
    arrive = {}
    todo = [(p, j) for j in range(NJ) for p in range(8)]
    ends = [(q, j) for j in range(NJ) for q in range(2)]
    done = set()
    while todo or events or ends:
        while events and events[0][0] <= now:
            _, name, arg = events.pop(0)
            order.append((name, arg))
            if name == "a_done":
                a_ok.add(arg)
            if name == "b_done":
                b_ok.add(arg)
        best = None
        wake = events[0][0] if events else 1e9
        for q, j in ends:
            if (6 + q, j) not in done or (2 + q, j) not in arrive or (4 + q, j) not in arrive:
                continue
            at = max(arrive[(2 + q, j)], arrive[(4 + q, j)])
            if at <= now:
                best = ((1, 9, j, q), ("final", q, j))
                break
            wake = min(wake, at)
        for p, j in todo:
            if p not in a_ok or j not in b_ok:
                continue
            kind, q = p // 2, p % 2
            if kind == 1:
                if (q, j) not in arrive:
                    continue
                if arrive[(q, j)] > now:
                    wake = min(wake, arrive[(q, j)])
                    continue
            rank = (2, 0, j, p) if kind == 3 else (0, kind == 1, j, p)
            if best is None or rank < best[0]:
                best = (rank, ("unit", p, j))
        if best is None:
            now = wake
            continue
        name, p, j = best[1]
        if name == "final":
            ends.remove((p, j))
            order.append(("final", p, j))
            now += 0.25
            continue
        todo.remove((p, j))
        done.add((p, j))
        last = order[-1]
        if last[0] == "unit" and last[1] == p and last[2] + last[3] == j:
            order[-1] = ("unit", p, last[2], last[3] + 1)
        else:
            order.append(("unit", p, j, 1))
        now += unit_us
        if p < 6:
            link = max(link, now) + out_us
            arrive[(p, j)] = link + lag
    return order, now


def square_kernel(
    vec_ref, atoms_ref, lower_ref, upper_ref, w_hbm, base_hbm, o_ref,
    edges, t_ref, a, b, rf, rp, rm,
    w_sem, base_sem, edge_sem, snd, rcv,
    a2_sem, al_sem, ar_sem, af_sem, sb_sem, bl_sem, br_sem, bf_sem, rf_sem, rp_sem, rm_sem,
    a2_snd, ay_snd, sb_snd, b_snd, x_snd, own_sem,
):
    row = lax.axis_index("row")
    col = lax.axis_index("col")
    z, x, y, c = row // 4, row % 4, col // 2, col % 2
    mod = lambda v: (v + 4) % 4
    dev = lambda zz, xx, yy, cc: (zz * 4 + xx, yy * 2 + cc)
    zr, zl = dev(mod(z + 1), x, y, c), dev(mod(z - 1), x, y, c)
    yr, yl = dev(z, x, mod(y + 1), c), dev(z, x, mod(y - 1), c)
    xr, xl = dev(z, mod(x + 1), y, c), dev(z, mod(x - 1), y, c)
    sib = dev(z, x, y, 1 - c)

    def build(edge_ref, padded, emb, wide, sel, w, base, direct, mirror):
        w_copy = pltpu.make_async_copy(w_hbm, w, w_sem)
        base_copy = pltpu.make_async_copy(base_hbm, base, base_sem)
        w_copy.start()
        base_copy.start()

        barrier = pltpu.get_barrier_semaphore()
        for d in range(1, 8):
            pl.semaphore_signal(
                barrier, inc=1, device_id=(row, (col + d) % 8), device_id_type=MESH
            )
        for d in range(1, 16):
            pl.semaphore_signal(
                barrier, inc=1, device_id=((row + d) % 16, col), device_id_type=MESH
            )
        for d in range(1, 4):
            pl.semaphore_signal(
                barrier, inc=1, device_id=dev(z, mod(x + d), y, 1 - c), device_id_type=MESH
            )

        padded[...] = jnp.zeros((8, ORB), jnp.float32)
        padded[0:3, 0:8] = vec_ref[...]
        padded[3:5, 0:8] = atoms_ref[...].astype(jnp.float32)
        packed = padded[0:1, :]
        for n in range(1, 5):
            packed = packed + pltpu.roll(padded[n : n + 1, :], 8 * n, 1)
        edge_ref[...] = packed
        pl.semaphore_wait(barrier, 25)

        mine = row * 8 + col
        own = pltpu.make_async_copy(edge_ref, edges.at[pl.ds(mine, 1), :], edge_sem)
        own.start()
        copies = []
        for d in range(1, 8):
            copy = pltpu.make_async_remote_copy(
                src_ref=edge_ref, dst_ref=edges.at[pl.ds(mine, 1), :],
                send_sem=snd.at[d], recv_sem=rcv.at[d],
                device_id=(row, (col + d) % 8), device_id_type=MESH,
            )
            copy.start()
            copies.append(copy)
        own.wait()
        for d in range(1, 8):
            src = row * 8 + (col + 8 - d) % 8
            pltpu.make_async_remote_copy(
                src_ref=edge_ref, dst_ref=edges.at[pl.ds(src, 1), :],
                send_sem=snd.at[d], recv_sem=rcv.at[d],
                device_id=(row, (col + d) % 8), device_id_type=MESH,
            ).wait_recv()

        def group(r):
            return edges.at[pl.ds(pl.multiple_of(r * 8, 8), 8), :]

        for d in range(1, 16):
            copy = pltpu.make_async_remote_copy(
                src_ref=group(row), dst_ref=group(row),
                send_sem=snd.at[7 + d], recv_sem=rcv.at[7 + d],
                device_id=((row + d) % 16, col), device_id_type=MESH,
            )
            copy.start()
            copies.append(copy)
        for d in range(1, 16):
            src = (row + 16 - d) % 16
            pltpu.make_async_remote_copy(
                src_ref=group(src), dst_ref=group(src),
                send_sem=snd.at[7 + d], recv_sem=rcv.at[7 + d],
                device_id=((row + d) % 16, col), device_id_type=MESH,
            ).wait_recv()
        for copy in copies:
            copy.wait_send()

        fields = edges[...].T
        vx, vy, vz = fields[0:8], fields[8:16], fields[16:24]
        first, second = fields[24:32], fields[32:40]
        radius = jnp.sqrt(vx * vx + vy * vy + vz * vz + 0.25)
        ux, uy, uz = vx / radius, vy / radius, vz / radius
        harmonics = [
            None, ux, uy, uz, ux * uy, uy * uz, uz * ux, ux * ux - uy * uy, 3.0 * uz * uz - 1.0
        ]
        for k in range(NR):
            scaled = (radius - (1.0 + 0.3 * k)) / 0.5
            radial = jnp.exp(-(scaled * scaled))
            for m in range(9):
                f = 9 * k + m
                emb[f * 8 : f * 8 + 8, :] = radial if m == 0 else radial * harmonics[m]
        number = lax.broadcasted_iota(jnp.int32, (PAIRS, ORB), 0)
        upper_atom = jnp.zeros((PAIRS, ORB), jnp.int32)
        for n in range(1, RB):
            upper_atom = upper_atom + jnp.where(number >= CB * n, 1, 0)
        pair = (row * RB + upper_atom) * NB + col * CB + number - CB * upper_atom
        pair = pair.astype(jnp.float32)
        forward = first * float(NB) + second
        backward = second * float(NB) + first
        for i in range(8):
            lanes = slice(i * ORB, (i + 1) * ORB)
            sel[0:PAIRS, lanes] = jnp.where(forward[i : i + 1] == pair, 1.0, 0.0)
            sel[PAIRS : 2 * PAIRS, lanes] = jnp.where(backward[i : i + 1] == pair, 1.0, 0.0)
            wide[:, lanes] = emb[pl.ds(i, FEAT, stride=8), :]
        coefficient = lax.dot_general(
            sel[...], wide[...], (((1,), (1,)), ((), ())),
            precision=lax.Precision.HIGHEST, preferred_element_type=jnp.float32,
        ).astype(jnp.bfloat16)

        w_copy.wait()

        def expand(n, carry):
            start = pl.multiple_of(n * 8 * ORB, 8 * ORB)
            part = jnp.dot(
                coefficient, w[:, pl.ds(start, 8 * ORB)], preferred_element_type=jnp.float32
            )
            place = pl.ds(pl.multiple_of(n * 8, 8), 8)
            direct[:, place, :] = part[:PAIRS].reshape(PAIRS, 8, ORB)
            mirror[:, place, :] = part[PAIRS:].reshape(PAIRS, 8, ORB)
            return carry

        lax.fori_loop(0, ORB // 8, expand, 0)
        base_copy.wait()
        upper = upper_ref[0]
        scale = upper - lower_ref[0]
        on_diagonal = lax.broadcasted_iota(jnp.int32, (ORB, ORB), 0) == lax.broadcasted_iota(
            jnp.int32, (ORB, ORB), 1
        )

        def finish(i, carry):
            rows = pl.ds(pl.multiple_of(i * ORB, ORB), ORB)
            for k in range(CB):
                lanes = slice(k * ORB, (k + 1) * ORB)
                both = direct[i * CB + k] + mirror[i * CB + k].T
                both = both + base[rows, lanes].astype(jnp.float32)
                shift = jnp.where(row * RB + i == col * CB + k, upper, 0.0)
                moved = jnp.where(on_diagonal, shift, 0.0) - both
                t_ref[rows, lanes] = (moved / scale).astype(jnp.bfloat16)
            return carry

        lax.fori_loop(0, RB, finish, 0)

    f32 = jnp.float32
    pl.run_scoped(
        build,
        pltpu.VMEM((1, ORB), f32),
        pltpu.VMEM((8, ORB), f32),
        pltpu.VMEM((FEAT * 8, ORB), f32),
        pltpu.VMEM((FEAT, EDGES), f32),
        pltpu.VMEM((2 * PAIRS, EDGES), f32),
        pltpu.VMEM((FEAT, ORB * ORB), jnp.bfloat16),
        pltpu.VMEM((ROWS, COLS), jnp.bfloat16),
        pltpu.VMEM((PAIRS, ORB, ORB), f32),
        pltpu.VMEM((PAIRS, ORB, ORB), f32),
    )

    pending = []

    def remote(src, dst, snd, rcv, target):
        return pltpu.make_async_remote_copy(
            src_ref=src, dst_ref=dst, send_sem=snd, recv_sem=rcv,
            device_id=target, device_id_type=MESH,
        )

    def push(src, dst, snd, rcv, target):
        copy = remote(src, dst, snd, rcv, target)
        copy.start()
        pending.append((None, copy))

    def arrived(dst, rcv):
        remote(dst, dst, own_sem.at[1], rcv, sib).wait_recv()

    def exchange(r, h, q):
        kk = mod(x - r)
        active = (kk // 2) == c
        cols = pl.ds(pl.multiple_of((kk % 2) * ROWS, ROWS), ROWS)
        place = pl.ds(pl.multiple_of(y * ROWS, ROWS), ROWS)
        p = 2 * {0: 3, 2: 0, 1: 1 + h, 3: 2 - h}[r] + q
        for s in range(2):
            src = t_ref.at[pl.ds(h * HALF + q * QUART + s * SUB, SUB), cols]
            dst = a.at[p, pl.ds(h * QUART + s * SUB, SUB), place]
            snd, rcv = a2_snd.at[r, h, q, s], a2_sem.at[p, s]
            if r:
                copy = remote(src, dst, snd, rcv, dev(z, kk, y, h))
                pl.when(active)(copy.start)
                pending.append((active, copy))
            else:
                copy = remote(src, dst, snd, rcv, sib)
                cond = active & (c != h)
                pl.when(cond)(copy.start)
                pending.append((cond, copy))
                local = pltpu.make_async_copy(src, dst, rcv)
                pl.when(active & (c == h))(local.start)

    def a_piece(p, s, yy):
        return a.at[
            p,
            pl.ds(pl.multiple_of(c * QUART + s * SUB, SUB), SUB),
            pl.ds(pl.multiple_of(yy * ROWS, ROWS), ROWS),
        ]

    def a_half(p, yy, cc):
        return a.at[
            p,
            pl.ds(pl.multiple_of(cc * QUART, QUART), QUART),
            pl.ds(pl.multiple_of(yy * ROWS, ROWS), ROWS),
        ]

    def along(p, s, yy, snd, rcv, target):
        push(a_piece(p, s, yy), a_piece(p, s, yy), ay_snd.at[p, snd], rcv.at[p, s], target)

    def share(p, i, yy):
        push(a_half(p, yy, c), a_half(p, yy, c), sb_snd.at[p, i], sb_sem.at[p, i], sib)

    def a_own(p):
        arrived(a_piece(p, 0, y), a2_sem.at[p, 0])
        along(p, 0, y, 0, al_sem, yr)
        arrived(a_piece(p, 1, y), a2_sem.at[p, 1])
        along(p, 1, y, 1, ar_sem, yl)
        along(p, 1, y, 2, al_sem, yr)
        along(p, 0, y, 3, ar_sem, yl)
        share(p, 0, y)

    def a_relay(p):
        left, right = mod(y - 1), mod(y + 1)
        arrived(a_piece(p, 0, left), al_sem.at[p, 0])
        along(p, 0, left, 4, af_sem, yr)
        arrived(a_piece(p, 1, right), ar_sem.at[p, 1])
        along(p, 1, right, 5, af_sem, yl)

    def a_fwd(p):
        left, right = mod(y - 1), mod(y + 1)
        arrived(a_piece(p, 1, left), al_sem.at[p, 1])
        if p == 6:
            arrived(a_piece(p, 0, left), al_sem.at[p, 0])
        share(p, 1, left)
        arrived(a_piece(p, 0, right), ar_sem.at[p, 0])
        if p == 6:
            arrived(a_piece(p, 1, right), ar_sem.at[p, 1])
        share(p, 2, right)

    def a_late(p):
        left, right = mod(y - 1), mod(y + 1)
        along(p, 0, left, 4, af_sem, yr)
        along(p, 1, right, 5, af_sem, yl)

    def a_far(p):
        far = mod(y + 2)
        arrived(a_piece(p, 0, far), af_sem.at[p, 0])
        arrived(a_piece(p, 1, far), af_sem.at[p, 1])
        share(p, 3, far)

    def a_done(p):
        for i, yy in enumerate((y, mod(y - 1), mod(y + 1), mod(y + 2))):
            arrived(a_half(p, yy, 1 - c), sb_sem.at[p, i])

    def b_piece(j, s, zz):
        return b.at[pl.ds(pl.multiple_of(zz * ROWS + s * HALF, HALF), HALF), pl.ds(j * JW, JW)]

    def b_own(j):
        for i, (s, right) in enumerate(((0, True), (1, False), (1, True), (0, False))):
            src = t_ref.at[pl.ds(s * HALF, HALF), pl.ds(j * JW, JW)]
            rcv = bl_sem.at[j, s] if right else br_sem.at[j, s]
            push(src, b_piece(j, s, z), b_snd.at[j, i], rcv, zr if right else zl)

    def b_relay(j):
        left, right = mod(z - 1), mod(z + 1)
        arrived(b_piece(j, 0, left), bl_sem.at[j, 0])
        push(b_piece(j, 0, left), b_piece(j, 0, left), b_snd.at[j, 4], bf_sem.at[j, 0], zr)
        arrived(b_piece(j, 1, right), br_sem.at[j, 1])
        push(b_piece(j, 1, right), b_piece(j, 1, right), b_snd.at[j, 5], bf_sem.at[j, 1], zl)

    own_tile = b.at[pl.ds(pl.multiple_of(z * ROWS, ROWS), ROWS), :]
    own_copy = pltpu.make_async_copy(t_ref, own_tile, own_sem.at[0])

    def b_done(j):
        if j == 0:
            own_copy.wait()
        arrived(b_piece(j, 1, mod(z - 1)), bl_sem.at[j, 1])
        arrived(b_piece(j, 0, mod(z + 1)), br_sem.at[j, 0])
        for s in range(2):
            arrived(b_piece(j, s, mod(z + 2)), bf_sem.at[j, s])

    def block(ref, q, h, j):
        return ref.at[pl.ds(q * HALF + h * QUART, QUART), pl.ds(j * JW, JW)]

    def unit(s0, s1, s2, out, p, first, count):
        kind, q = p // 2, p % 2
        rows = pl.ds(q * HALF, HALF)
        source = (s0, s1, s2, None)[kind]

        def step(j):
            cols = pl.ds(j * JW if count == 1 else pl.multiple_of(j * JW, JW), JW)
            if kind == 1:
                for h in range(2):
                    arrived(block(rf, q, h, j), rf_sem.at[q, h, j])
            acc = jnp.dot(a[p], b[:, cols], preferred_element_type=jnp.float32)
            if kind == 1:
                acc = acc + rf[rows, cols].astype(jnp.float32)
            if kind == 3:
                for h in range(2):
                    out[pl.ds(h * HALF + q * QUART, QUART), cols] = acc[h * QUART : (h + 1) * QUART]
                return
            source[rows, cols] = acc.astype(jnp.bfloat16)
            for h in range(2):
                reduce_copy(source, p, h, j).start()

        if count == 1:
            step(first)
        else:
            lax.fori_loop(first, first + count, lambda j, carry: (step(j), carry)[1], 0)

    def reduce_copy(source, p, h, j):
        kind, q = p // 2, p % 2
        target = xr if (h == 0) == (kind < 2) else xl
        into, sem = (rf, rf_sem) if kind == 0 else (rp, rp_sem) if target is xr else (rm, rm_sem)
        return remote(
            block(source, q, h, j), block(into, q, h, j), x_snd.at[p, h, j], sem.at[q, h, j], target
        )

    def final(out, q, j):
        cols = pl.ds(j * JW, JW)
        rows = pl.ds(q * HALF, HALF)
        for h in range(2):
            arrived(block(rp, q, h, j), rp_sem.at[q, h, j])
            arrived(block(rm, q, h, j), rm_sem.at[q, h, j])
        for h in range(2):
            rows = pl.ds(q * HALF + h * QUART, QUART)
            into = pl.ds(h * HALF + q * QUART, QUART)
            out[into, cols] = (
                out[into, cols] + rp[rows, cols].astype(jnp.float32) + rm[rows, cols].astype(jnp.float32)
            )

    def work(s0, s1, s2):
        out = o_ref
        for r, hs in ((0, (0, 1)), (1, (1,)), (3, (0,)), (2, (0, 1)), (1, (0,)), (3, (1,))):
            for q in range(2):
                for h in hs:
                    exchange(r, h, q)
        own_copy.start()
        steps = {
            "a_own": a_own, "a_relay": a_relay, "a_fwd": a_fwd, "a_far": a_far, "a_done": a_done,
            "b_own": b_own, "b_relay": b_relay, "b_done": b_done,
        }
        for name, *args in plan()[0]:
            if name == "a_relay" and args == [6]:
                a_late(6)
            elif name == "unit":
                unit(s0, s1, s2, out, *args)
            elif name == "final":
                final(out, *args)
            else:
                steps[name](*args)
        for cond, copy in pending:
            if cond is None:
                copy.wait_send()
            else:
                pl.when(cond)(copy.wait_send)
        for p in range(6):
            for h in range(2):
                for j in range(NJ):
                    reduce_copy((s0, s1, s2)[p // 2], p, h, j).wait_send()

    tiles = pltpu.VMEM((ROWS, COLS), jnp.bfloat16)
    pl.run_scoped(work, tiles, tiles, tiles)


def square(vec, atoms, lower, upper, weight, base):
    dma = pltpu.SemaphoreType.DMA
    bf = jnp.bfloat16
    return pl.pallas_call(
        square_kernel,
        out_shape=pltpu.VMEM((ROWS, COLS), jnp.float32),
        in_specs=[
            pl.BlockSpec(memory_space=pltpu.VMEM),
            pl.BlockSpec(memory_space=pltpu.VMEM),
            pl.BlockSpec(memory_space=pltpu.SMEM),
            pl.BlockSpec(memory_space=pltpu.SMEM),
            pl.BlockSpec(memory_space=pl.ANY),
            pl.BlockSpec(memory_space=pl.ANY),
        ],
        out_specs=pl.BlockSpec(memory_space=pltpu.VMEM),
        scratch_shapes=[
            pltpu.VMEM((ORB, ORB), jnp.float32),
            pltpu.VMEM((ROWS, COLS), bf),
            pltpu.VMEM((8, HALF, K), bf),
            pltpu.VMEM((K, COLS), bf),
            pltpu.VMEM((ROWS, COLS), bf),
            pltpu.VMEM((ROWS, COLS), bf),
            pltpu.VMEM((ROWS, COLS), bf),
            dma, dma, dma, dma((23,)), dma((23,)),
            dma((8, 2)), dma((8, 2)), dma((8, 2)), dma((8, 2)), dma((8, 4)),
            dma((NJ, 2)), dma((NJ, 2)), dma((NJ, 2)),
            dma((2, 2, NJ)), dma((2, 2, NJ)), dma((2, 2, NJ)),
            dma((4, 2, 2, 2)), dma((8, 6)), dma((8, 4)), dma((NJ, 6)), dma((6, 2, NJ)),
            dma((2,)),
        ],
        compiler_params=pltpu.CompilerParams(
            collective_id=0, has_side_effects=True, vmem_limit_bytes=56 * 2**20
        ),
        name="square",
    )(vec, atoms, lower, upper, weight, base)


def shards(edge_vec, edge_atoms, block_weight, base_hamiltonian, lower_bound, upper_bound):
    return square(
        edge_vec, edge_atoms, lower_bound, upper_bound, block_weight, base_hamiltonian
    )


def solution(mesh):
    return jax.shard_map(
        shards,
        mesh=mesh,
        in_specs=(P(None, ("row", "col")), P(None, ("row", "col")), P(), P("row", "col"), P(), P()),
        out_specs=P("row", "col"),
        check_vma=False,
    )
```

```python
import jax
import jax.numpy as jnp
from jax import lax
from jax.experimental import pallas as pl
from jax.experimental.pallas import tpu as pltpu
from jax.sharding import PartitionSpec as P

ORB = 128
NR = 16
RB = 6
CB = 12
NB = 96
FEAT = 144
EDGES = 1024
PADDED = 40
ROWS = 768
COLS = 1536
K = 3072
NJ = 6
JW = COLS // NJ
HALF = ROWS // 2
QUART = ROWS // 4
SUB = ROWS // 8
MESH = pl.DeviceIdType.MESH


def plan():
    z_period, y_period = 12.7, 9.5
    z_lead, y_lead, x_lead = -0.5, 5.2, 24.0
    unit_us, out_us, lag = 1.05, 2.15, 3.0
    ring = [4, 5, 0, 1, 2, 3, 6, 7]
    events = [(y_lead, "a_own", ring[0])]
    for j in range(NJ):
        start = z_lead + z_period * j
        events.append((start + 5.7, "b_right", j))
        if j + 1 < NJ:
            events.append((start + 5.8, "b_own", j + 1))
        events.append((start + (10.4 if j == 0 else 5.75), "b_left", j))
        events.append((start + z_period + 2.5, "b_done", j))
    for i, p in enumerate(ring):
        start = y_lead + y_period * i
        events.append((start + 5.0, "a_relay", p))
        if i + 1 < len(ring):
            events.append((start + 5.1, "a_own", ring[i + 1]))
        events.append((start + 8.3, "a_fwd", p))
        events.append((start + y_period + 2.0, "a_far", p))
        events.append((start + y_period + 4.5, "a_done", p))
    events.sort(key=lambda e: e[0])
    order = []
    now, link = 0.0, x_lead
    a_ok, b_ok = set(), set()
    arrive = {}
    todo = [(p, j) for j in range(NJ) for p in range(8)]
    ends = [(q, j) for j in range(NJ) for q in range(2)]
    done = set()
    while todo or events or ends:
        while events and events[0][0] <= now:
            _, name, arg = events.pop(0)
            order.append((name, arg))
            if name == "a_done":
                a_ok.add(arg)
            if name == "b_done":
                b_ok.add(arg)
        best = None
        wake = events[0][0] if events else 1e9
        for q, j in ends:
            if (6 + q, j) not in done or (2 + q, j) not in arrive or (4 + q, j) not in arrive:
                continue
            at = max(arrive[(2 + q, j)], arrive[(4 + q, j)])
            if at <= now:
                best = ((1, 9, j, q), ("final", q, j))
                break
            wake = min(wake, at)
        for p, j in todo:
            if p not in a_ok or j not in b_ok:
                continue
            kind, q = p // 2, p % 2
            if kind == 1:
                if (q, j) not in arrive:
                    continue
                if arrive[(q, j)] > now:
                    wake = min(wake, arrive[(q, j)])
                    continue
            rank = (2, 0, j, p) if kind == 3 else (0, kind == 1, j, p)
            if best is None or rank < best[0]:
                best = (rank, ("unit", p, j))
        if best is None:
            now = wake
            continue
        name, p, j = best[1]
        if name == "final":
            ends.remove((p, j))
            order.append(("final", p, j))
            now += 0.25
            continue
        todo.remove((p, j))
        done.add((p, j))
        last = order[-1]
        if last[0] == "unit" and last[1] == p and last[2] + last[3] == j:
            order[-1] = ("unit", p, last[2], last[3] + 1)
        else:
            order.append(("unit", p, j, 1))
        now += unit_us
        if p < 6:
            link = max(link, now) + out_us
            arrive[(p, j)] = link + lag
    return order, now


def square_kernel(
    vec_ref, atoms_ref, lower_ref, upper_ref, w_hbm, base_hbm, o_ref,
    edges, t_ref, a, b, rf, rp, rm,
    w_sem, base_sem, edge_sem, snd, rcv,
    a2_sem, al_sem, ar_sem, af_sem, sb_sem, bl_sem, br_sem, bf_sem, rf_sem, rp_sem, rm_sem,
    a2_snd, ay_snd, sb_snd, b_snd, x_snd, own_sem,
):
    row = lax.axis_index("row")
    col = lax.axis_index("col")
    z, x, y, c = row // 4, row % 4, col // 2, col % 2
    mod = lambda v: (v + 4) % 4
    dev = lambda zz, xx, yy, cc: (zz * 4 + xx, yy * 2 + cc)
    zr, zl = dev(mod(z + 1), x, y, c), dev(mod(z - 1), x, y, c)
    yr, yl = dev(z, x, mod(y + 1), c), dev(z, x, mod(y - 1), c)
    xr, xl = dev(z, mod(x + 1), y, c), dev(z, mod(x - 1), y, c)
    sib = dev(z, x, y, 1 - c)

    pending = []

    def remote(src, dst, snd, rcv, target):
        return pltpu.make_async_remote_copy(
            src_ref=src, dst_ref=dst, send_sem=snd, recv_sem=rcv,
            device_id=target, device_id_type=MESH,
        )

    def push(src, dst, snd, rcv, target):
        copy = remote(src, dst, snd, rcv, target)
        copy.start()
        pending.append(copy)

    def arrived(dst, rcv):
        remote(dst, dst, own_sem.at[NJ], rcv, sib).wait_recv()

    def exchange(r, h, q, sent=False):
        kk = mod(x - r)
        active = (kk // 2) == c
        cols = pl.ds(pl.multiple_of((kk % 2) * ROWS, ROWS), ROWS)
        place = pl.ds(pl.multiple_of(y * ROWS, ROWS), ROWS)
        p = 2 * {0: 3, 2: 0, 1: 1 + h, 3: 2 - h}[r] + q
        for s in range(2):
            src = t_ref.at[pl.ds(h * HALF + q * QUART + s * SUB, SUB), cols]
            dst = a.at[p, pl.ds(h * QUART + s * SUB, SUB), place]
            snd, rcv = a2_snd.at[r, h, q, s], a2_sem.at[p, s]
            if r:
                copy = remote(src, dst, snd, rcv, dev(z, kk, y, h))
                pl.when(active)(copy.wait_send if sent else copy.start)
            else:
                copy = remote(src, dst, snd, rcv, sib)
                pl.when(active & (c != h))(copy.wait_send if sent else copy.start)
                if not sent:
                    local = pltpu.make_async_copy(src, dst, rcv)
                    pl.when(active & (c == h))(local.start)

    def a_piece(p, s, yy):
        return a.at[
            p,
            pl.ds(pl.multiple_of(c * QUART + s * SUB, SUB), SUB),
            pl.ds(pl.multiple_of(yy * ROWS, ROWS), ROWS),
        ]

    def a_half(p, yy, cc):
        return a.at[
            p,
            pl.ds(pl.multiple_of(cc * QUART, QUART), QUART),
            pl.ds(pl.multiple_of(yy * ROWS, ROWS), ROWS),
        ]

    def along(p, s, yy, snd, rcv, target):
        push(a_piece(p, s, yy), a_piece(p, s, yy), ay_snd.at[p, snd], rcv.at[p, s], target)

    def share(p, i, yy):
        push(a_half(p, yy, c), a_half(p, yy, c), sb_snd.at[p, i], sb_sem.at[p, i], sib)

    def a_own(p):
        arrived(a_piece(p, 0, y), a2_sem.at[p, 0])
        along(p, 0, y, 0, al_sem, yr)
        arrived(a_piece(p, 1, y), a2_sem.at[p, 1])
        along(p, 1, y, 1, ar_sem, yl)
        along(p, 1, y, 2, al_sem, yr)
        along(p, 0, y, 3, ar_sem, yl)
        share(p, 0, y)

    def a_relay(p):
        left, right = mod(y - 1), mod(y + 1)
        arrived(a_piece(p, 0, left), al_sem.at[p, 0])
        along(p, 0, left, 4, af_sem, yr)
        arrived(a_piece(p, 1, right), ar_sem.at[p, 1])
        along(p, 1, right, 5, af_sem, yl)

    def a_fwd(p):
        left, right = mod(y - 1), mod(y + 1)
        arrived(a_piece(p, 1, left), al_sem.at[p, 1])
        share(p, 1, left)
        arrived(a_piece(p, 0, right), ar_sem.at[p, 0])
        share(p, 2, right)

    def a_far(p):
        far = mod(y + 2)
        arrived(a_piece(p, 0, far), af_sem.at[p, 0])
        arrived(a_piece(p, 1, far), af_sem.at[p, 1])
        share(p, 3, far)

    def a_done(p):
        for i, yy in enumerate((y, mod(y - 1), mod(y + 1), mod(y + 2))):
            arrived(a_half(p, yy, 1 - c), sb_sem.at[p, i])

    def b_piece(j, s, zz):
        return b.at[j, pl.ds(pl.multiple_of(zz * ROWS + s * HALF, HALF), HALF), :]

    def b_send(j, s, right, sent=False):
        src = t_ref.at[pl.ds(s * HALF, HALF), pl.ds(j * JW, JW)]
        rcv = bl_sem.at[j, s] if right else br_sem.at[j, s]
        copy = remote(src, b_piece(j, s, z), b_snd.at[j, 2 * s + right], rcv, zr if right else zl)
        (copy.wait_send if sent else copy.start)()

    def b_own(j):
        for s, right in ((0, True), (1, False), (1, True), (0, False)):
            b_send(j, s, right)

    def b_right(j):
        left = mod(z - 1)
        arrived(b_piece(j, 0, left), bl_sem.at[j, 0])
        push(b_piece(j, 0, left), b_piece(j, 0, left), b_snd.at[j, 4], bf_sem.at[j, 0], zr)

    def b_left(j):
        right = mod(z + 1)
        arrived(b_piece(j, 1, right), br_sem.at[j, 1])
        push(b_piece(j, 1, right), b_piece(j, 1, right), b_snd.at[j, 5], bf_sem.at[j, 1], zl)

    def own_copy(j):
        rows = pl.ds(pl.multiple_of(z * ROWS, ROWS), ROWS)
        return pltpu.make_async_copy(t_ref.at[:, pl.ds(j * JW, JW)], b.at[j, rows, :], own_sem.at[j])

    def b_done(j):
        own_copy(j).wait()
        arrived(b_piece(j, 1, mod(z - 1)), bl_sem.at[j, 1])
        arrived(b_piece(j, 0, mod(z + 1)), br_sem.at[j, 0])
        for s in range(2):
            arrived(b_piece(j, s, mod(z + 2)), bf_sem.at[j, s])

    def block(ref, q, h, j):
        return ref.at[j, pl.ds(q * HALF + h * QUART, QUART), :]

    def unit(s0, s1, s2, out, p, first, count):
        kind, q = p // 2, p % 2
        rows = pl.ds(q * HALF, HALF)
        source = (s0, s1, s2, None)[kind]

        def step(j):
            cols = pl.ds(j * JW if count == 1 else pl.multiple_of(j * JW, JW), JW)
            if kind == 1:
                for h in range(2):
                    arrived(block(rf, q, h, j), rf_sem.at[q, h, j])
            acc = jnp.dot(a[p], b[j], preferred_element_type=jnp.float32)
            if kind == 1:
                acc = acc + rf[j, rows, :].astype(jnp.float32)
            if kind == 3:
                for h in range(2):
                    out[pl.ds(h * HALF + q * QUART, QUART), cols] = acc[h * QUART : (h + 1) * QUART]
                return
            source[j, rows, :] = acc.astype(jnp.bfloat16)
            for h in range(2):
                reduce_copy(source, p, h, j).start()

        if count == 1:
            step(first)
        else:
            lax.fori_loop(first, first + count, lambda j, carry: (step(j), carry)[1], 0)

    def reduce_copy(source, p, h, j):
        kind, q = p // 2, p % 2
        target = xr if (h == 0) == (kind < 2) else xl
        into, sem = (rf, rf_sem) if kind == 0 else (rp, rp_sem) if target is xr else (rm, rm_sem)
        return remote(
            block(source, q, h, j), block(into, q, h, j), x_snd.at[p, h, j], sem.at[q, h, j], target
        )

    def final(out, q, j):
        cols = pl.ds(j * JW, JW)
        rows = pl.ds(q * HALF, HALF)
        for h in range(2):
            arrived(block(rp, q, h, j), rp_sem.at[q, h, j])
            arrived(block(rm, q, h, j), rm_sem.at[q, h, j])
        for h in range(2):
            rows = pl.ds(q * HALF + h * QUART, QUART)
            into = pl.ds(h * HALF + q * QUART, QUART)
            out[into, cols] = (
                out[into, cols] + rp[j, rows, :].astype(jnp.float32) + rm[j, rows, :].astype(jnp.float32)
            )

    def build(edge_ref, padded, emb, wide, sel, w, base, direct, mirror):
        w_copy = pltpu.make_async_copy(w_hbm, w, w_sem)
        base_copy = pltpu.make_async_copy(base_hbm, base, base_sem)
        w_copy.start()
        base_copy.start()

        barrier = pltpu.get_barrier_semaphore()
        for d in range(1, 8):
            pl.semaphore_signal(
                barrier, inc=1, device_id=(row, (col + d) % 8), device_id_type=MESH
            )
        for d in range(1, 16):
            pl.semaphore_signal(
                barrier, inc=1, device_id=((row + d) % 16, col), device_id_type=MESH
            )
        for d in range(1, 4):
            pl.semaphore_signal(
                barrier, inc=1, device_id=dev(z, mod(x + d), y, 1 - c), device_id_type=MESH
            )

        padded[...] = jnp.zeros((8, ORB), jnp.float32)
        padded[0:3, 0:8] = vec_ref[...]
        padded[3:5, 0:8] = atoms_ref[...].astype(jnp.float32)
        packed = padded[0:1, :]
        for n in range(1, 5):
            packed = packed + pltpu.roll(padded[n : n + 1, :], 8 * n, 1)
        edge_ref[...] = packed
        pl.semaphore_wait(barrier, 25)

        mine = row * 8 + col
        own = pltpu.make_async_copy(edge_ref, edges.at[pl.ds(mine, 1), :], edge_sem)
        own.start()
        copies = []
        for d in range(1, 8):
            copy = pltpu.make_async_remote_copy(
                src_ref=edge_ref, dst_ref=edges.at[pl.ds(mine, 1), :],
                send_sem=snd.at[d], recv_sem=rcv.at[d],
                device_id=(row, (col + d) % 8), device_id_type=MESH,
            )
            copy.start()
            copies.append(copy)
        own.wait()
        for d in range(1, 8):
            src = row * 8 + (col + 8 - d) % 8
            pltpu.make_async_remote_copy(
                src_ref=edge_ref, dst_ref=edges.at[pl.ds(src, 1), :],
                send_sem=snd.at[d], recv_sem=rcv.at[d],
                device_id=(row, (col + d) % 8), device_id_type=MESH,
            ).wait_recv()

        def group(r):
            return edges.at[pl.ds(pl.multiple_of(r * 8, 8), 8), :]

        for d in range(1, 16):
            copy = pltpu.make_async_remote_copy(
                src_ref=group(row), dst_ref=group(row),
                send_sem=snd.at[7 + d], recv_sem=rcv.at[7 + d],
                device_id=((row + d) % 16, col), device_id_type=MESH,
            )
            copy.start()
            copies.append(copy)
        for d in range(1, 16):
            src = (row + 16 - d) % 16
            pltpu.make_async_remote_copy(
                src_ref=group(src), dst_ref=group(src),
                send_sem=snd.at[7 + d], recv_sem=rcv.at[7 + d],
                device_id=((row + d) % 16, col), device_id_type=MESH,
            ).wait_recv()
        for copy in copies:
            copy.wait_send()

        fields = edges[...].T
        vx, vy, vz = fields[0:8], fields[8:16], fields[16:24]
        first, second = fields[24:32], fields[32:40]
        radius = jnp.sqrt(vx * vx + vy * vy + vz * vz + 0.25)
        ux, uy, uz = vx / radius, vy / radius, vz / radius
        harmonics = [
            None, ux, uy, uz, ux * uy, uy * uz, uz * ux, ux * ux - uy * uy, 3.0 * uz * uz - 1.0
        ]
        for k in range(NR):
            scaled = (radius - (1.0 + 0.3 * k)) / 0.5
            radial = jnp.exp(-(scaled * scaled))
            for m in range(9):
                f = 9 * k + m
                emb[f * 8 : f * 8 + 8, :] = radial if m == 0 else radial * harmonics[m]
        number = lax.broadcasted_iota(jnp.int32, (PADDED, ORB), 0)
        upper_atom = jnp.zeros((PADDED, ORB), jnp.int32)
        for n in range(1, RB):
            upper_atom = upper_atom + jnp.where(number >= CB * n, 1, 0)
        pair = (row * RB + upper_atom) * NB + col * CB + number - CB * upper_atom
        pair = pair.astype(jnp.float32)
        forward = first * float(NB) + second
        backward = second * float(NB) + first
        for i in range(8):
            lanes = slice(i * ORB, (i + 1) * ORB)
            for h in range(2):
                wanted = pair + float(h * RB // 2 * NB)
                at = 2 * PADDED * h
                sel[at : at + PADDED, lanes] = jnp.where(forward[i : i + 1] == wanted, 1.0, 0.0)
                sel[at + PADDED : at + 2 * PADDED, lanes] = jnp.where(
                    backward[i : i + 1] == wanted, 1.0, 0.0
                )
            wide[:, lanes] = emb[pl.ds(i, FEAT, stride=8), :]
        coefficient = lax.dot_general(
            sel[...], wide[...], (((1,), (1,)), ((), ())),
            precision=lax.Precision.HIGHEST, preferred_element_type=jnp.float32,
        ).astype(jnp.bfloat16)

        w_copy.wait()

        base_copy.wait()
        upper = upper_ref[0]
        scale = upper - lower_ref[0]
        on_diagonal = lax.broadcasted_iota(jnp.int32, (ORB, ORB), 0) == lax.broadcasted_iota(
            jnp.int32, (ORB, ORB), 1
        )

        def expand(n, carry):
            start = pl.multiple_of(n * 8 * ORB, 8 * ORB)
            part = jnp.dot(
                coefficient, w[:, pl.ds(start, 8 * ORB)], preferred_element_type=jnp.float32
            )
            place = pl.ds(pl.multiple_of(n * 8, 8), 8)
            for h in range(2):
                at = 2 * PADDED * h
                direct[h, :, place, :] = part[at : at + PADDED].reshape(PADDED, 8, ORB)
                at = at + PADDED
                mirror[h, :, place, :] = part[at : at + PADDED].reshape(PADDED, 8, ORB)
            return carry

        lax.fori_loop(0, ORB // 8, expand, 0)
        inverse = 1.0 / scale

        def half_tile(h):
            def finish(i, carry):
                rows = pl.ds(pl.multiple_of(h * HALF + i * ORB, ORB), ORB)
                for k in range(CB):
                    lanes = slice(k * ORB, (k + 1) * ORB)
                    both = direct[h, i * CB + k] + mirror[h, i * CB + k].T
                    both = both + base[rows, lanes].astype(jnp.float32)
                    atom = row * RB + h * (RB // 2) + i
                    shift = jnp.where(atom == col * CB + k, upper, 0.0)
                    moved = jnp.where(on_diagonal, shift, 0.0) - both
                    t_ref[rows, lanes] = (moved * inverse).astype(jnp.bfloat16)
                return carry

            lax.fori_loop(0, RB // 2, finish, 0)

        half_tile(0)
        for r, h, q in ((3, 0, 0), (3, 0, 1), (2, 0, 0)):
            exchange(r, h, q)
        b_send(0, 0, True)
        b_send(0, 0, False)
        for q in range(2):
            exchange(0, 0, q)
        half_tile(1)
        for r, h, q in (
            (1, 1, 0), (1, 1, 1), (2, 1, 0), (2, 0, 1), (2, 1, 1),
            (1, 0, 0), (3, 1, 0), (1, 0, 1), (3, 1, 1),
        ):
            exchange(r, h, q)
        b_send(0, 1, True)
        b_send(0, 1, False)
        for q in range(2):
            exchange(0, 1, q)

    f32 = jnp.float32
    pl.run_scoped(
        build,
        pltpu.VMEM((1, ORB), f32),
        pltpu.VMEM((8, ORB), f32),
        pltpu.VMEM((FEAT * 8, ORB), f32),
        pltpu.VMEM((FEAT, EDGES), f32),
        pltpu.VMEM((4 * PADDED, EDGES), f32),
        pltpu.VMEM((FEAT, ORB * ORB), jnp.bfloat16),
        pltpu.VMEM((ROWS, COLS), jnp.bfloat16),
        pltpu.VMEM((2, PADDED, ORB, ORB), f32),
        pltpu.VMEM((2, PADDED, ORB, ORB), f32),
    )

    def work(s0, s1, s2):
        out = o_ref
        for j in range(NJ):
            own_copy(j).start()
        steps = {
            "a_own": a_own, "a_relay": a_relay, "a_fwd": a_fwd, "a_far": a_far, "a_done": a_done,
            "b_own": b_own, "b_right": b_right, "b_left": b_left, "b_done": b_done,
        }
        for name, *args in plan()[0]:
            if name == "unit":
                unit(s0, s1, s2, out, *args)
            elif name == "final":
                final(out, *args)
            else:
                steps[name](*args)
        for copy in pending:
            copy.wait_send()
        for i in range(16):
            exchange(i // 4, i // 2 % 2, i % 2, True)
        for i in range(4 * NJ):
            b_send(i // 4, i // 2 % 2, i % 2 == 0, True)
        for p in range(6):
            for h in range(2):
                for j in range(NJ):
                    reduce_copy((s0, s1, s2)[p // 2], p, h, j).wait_send()

    tiles = pltpu.VMEM((NJ, ROWS, JW), jnp.bfloat16)
    pl.run_scoped(work, tiles, tiles, tiles)


def square(vec, atoms, lower, upper, weight, base):
    dma = pltpu.SemaphoreType.DMA
    bf = jnp.bfloat16
    return pl.pallas_call(
        square_kernel,
        out_shape=pltpu.VMEM((ROWS, COLS), jnp.float32),
        in_specs=[
            pl.BlockSpec(memory_space=pltpu.VMEM),
            pl.BlockSpec(memory_space=pltpu.VMEM),
            pl.BlockSpec(memory_space=pltpu.SMEM),
            pl.BlockSpec(memory_space=pltpu.SMEM),
            pl.BlockSpec(memory_space=pl.ANY),
            pl.BlockSpec(memory_space=pl.ANY),
        ],
        out_specs=pl.BlockSpec(memory_space=pltpu.VMEM),
        scratch_shapes=[
            pltpu.VMEM((ORB, ORB), jnp.float32),
            pltpu.VMEM((ROWS, COLS), bf),
            pltpu.VMEM((8, HALF, K), bf),
            pltpu.VMEM((NJ, K, JW), bf),
            pltpu.VMEM((NJ, ROWS, JW), bf),
            pltpu.VMEM((NJ, ROWS, JW), bf),
            pltpu.VMEM((NJ, ROWS, JW), bf),
            dma, dma, dma, dma((23,)), dma((23,)),
            dma((8, 2)), dma((8, 2)), dma((8, 2)), dma((8, 2)), dma((8, 4)),
            dma((NJ, 2)), dma((NJ, 2)), dma((NJ, 2)),
            dma((2, 2, NJ)), dma((2, 2, NJ)), dma((2, 2, NJ)),
            dma((4, 2, 2, 2)), dma((8, 6)), dma((8, 4)), dma((NJ, 6)), dma((6, 2, NJ)),
            dma((NJ + 1,)),
        ],
        compiler_params=pltpu.CompilerParams(
            collective_id=0, has_side_effects=True, vmem_limit_bytes=56 * 2**20
        ),
        name="square",
    )(vec, atoms, lower, upper, weight, base)


def shards(edge_vec, edge_atoms, block_weight, base_hamiltonian, lower_bound, upper_bound):
    return square(
        edge_vec, edge_atoms, lower_bound, upper_bound, block_weight, base_hamiltonian
    )


def solution(mesh):
    return jax.shard_map(
        shards,
        mesh=mesh,
        in_specs=(P(None, ("row", "col")), P(None, ("row", "col")), P(), P("row", "col"), P(), P()),
        out_specs=P("row", "col"),
        check_vma=False,
    )
```

```python
import jax
import jax.numpy as jnp
from jax import lax
from jax.experimental import pallas as pl
from jax.experimental.pallas import tpu as pltpu
from jax.sharding import PartitionSpec as P

ORB = 128
NR = 16
RB = 6
CB = 12
NB = 96
FEAT = 144
EDGES = 1024
PADDED = 40
ROWS = 768
COLS = 1536
K = 3072
NJ = 6
JW = COLS // NJ
HALF = ROWS // 2
QUART = ROWS // 4
SUB = ROWS // 8
MESH = pl.DeviceIdType.MESH
HOPS = (0, 1, 2, 1)
COL_ORDER = sorted(range(1, 8), key=lambda d: -HOPS[d // 2])
ROW_ORDER = sorted(range(1, 16), key=lambda d: -HOPS[d // 4] - HOPS[d % 4])


def plan():
    z_period, y_period = 12.7, 9.5
    z_lead, y_lead, x_lead = -0.5, 5.2, 24.0
    unit_us, out_us, lag = 1.05, 2.15, 3.0
    ring = [4, 5, 0, 1, 2, 3, 6, 7]
    events = [(y_lead, "a_own", ring[0])]
    for j in range(NJ):
        start = z_lead + z_period * j
        events.append((start + 5.7, "b_right", j))
        if j + 1 < NJ:
            events.append((start + 5.8, "b_own", j + 1))
        events.append((start + (10.4 if j == 0 else 5.75), "b_left", j))
        events.append((start + z_period + 2.5, "b_done", j))
    for i, p in enumerate(ring):
        start = y_lead + y_period * i
        events.append((start + 5.0, "a_relay", p))
        if i + 1 < len(ring):
            events.append((start + 5.1, "a_own", ring[i + 1]))
        events.append((start + 8.3, "a_fwd", p))
        events.append((start + y_period + 2.0, "a_far", p))
        events.append((start + y_period + 4.5, "a_done", p))
    events.sort(key=lambda e: e[0])
    order = []
    now, link = 0.0, x_lead
    a_ok, b_ok = set(), set()
    arrive = {}
    todo = [(p, j) for j in range(NJ) for p in range(8)]
    ends = [(q, j) for j in range(NJ) for q in range(2)]
    done = set()
    while todo or events or ends:
        while events and events[0][0] <= now:
            _, name, arg = events.pop(0)
            order.append((name, arg))
            if name == "a_done":
                a_ok.add(arg)
            if name == "b_done":
                b_ok.add(arg)
        best = None
        wake = events[0][0] if events else 1e9
        for q, j in ends:
            if (6 + q, j) not in done or (2 + q, j) not in arrive or (4 + q, j) not in arrive:
                continue
            at = max(arrive[(2 + q, j)], arrive[(4 + q, j)])
            if at <= now:
                best = ((1, 9, j, q), ("final", q, j))
                break
            wake = min(wake, at)
        for p, j in todo:
            if p not in a_ok or j not in b_ok:
                continue
            kind, q = p // 2, p % 2
            if kind == 1:
                if (q, j) not in arrive:
                    continue
                if arrive[(q, j)] > now:
                    wake = min(wake, arrive[(q, j)])
                    continue
            rank = (2, 0, j, p) if kind == 3 else (0, kind == 1, j, p)
            if best is None or rank < best[0]:
                best = (rank, ("unit", p, j))
        if best is None:
            now = wake
            continue
        name, p, j = best[1]
        if name == "final":
            ends.remove((p, j))
            order.append(("final", p, j))
            now += 0.25
            continue
        todo.remove((p, j))
        done.add((p, j))
        last = order[-1]
        if last[0] == "unit" and last[1] == p and last[2] + last[3] == j:
            order[-1] = ("unit", p, last[2], last[3] + 1)
        else:
            order.append(("unit", p, j, 1))
        now += unit_us
        if p < 6:
            link = max(link, now) + out_us
            arrive[(p, j)] = link + lag
    return order, now


def square_kernel(
    vec_ref, atoms_ref, lower_ref, upper_ref, w_hbm, base_hbm, o_ref,
    edges, t_ref, a, b, rf, rp, rm,
    w_sem, base_sem, edge_sem, snd, rcv,
    a2_sem, al_sem, ar_sem, af_sem, sb_sem, bl_sem, br_sem, bf_sem, rf_sem, rp_sem, rm_sem,
    a2_snd, ay_snd, sb_snd, b_snd, x_snd, own_sem,
):
    row = lax.axis_index("row")
    col = lax.axis_index("col")
    z, x, y, c = row // 4, row % 4, col // 2, col % 2
    mod = lambda v: (v + 4) % 4
    dev = lambda zz, xx, yy, cc: (zz * 4 + xx, yy * 2 + cc)
    zr, zl = dev(mod(z + 1), x, y, c), dev(mod(z - 1), x, y, c)
    yr, yl = dev(z, x, mod(y + 1), c), dev(z, x, mod(y - 1), c)
    xr, xl = dev(z, mod(x + 1), y, c), dev(z, mod(x - 1), y, c)
    sib = dev(z, x, y, 1 - c)

    pending = []

    def remote(src, dst, snd, rcv, target):
        return pltpu.make_async_remote_copy(
            src_ref=src, dst_ref=dst, send_sem=snd, recv_sem=rcv,
            device_id=target, device_id_type=MESH,
        )

    def push(src, dst, snd, rcv, target):
        copy = remote(src, dst, snd, rcv, target)
        copy.start()
        pending.append(copy)

    def arrived(dst, rcv):
        remote(dst, dst, own_sem.at[NJ], rcv, sib).wait_recv()

    def exchange(r, h, q, sent=False):
        kk = mod(x - r)
        active = (kk // 2) == c
        cols = pl.ds(pl.multiple_of((kk % 2) * ROWS, ROWS), ROWS)
        place = pl.ds(pl.multiple_of(y * ROWS, ROWS), ROWS)
        p = 2 * {0: 3, 2: 0, 1: 1 + h, 3: 2 - h}[r] + q
        for s in range(2):
            src = t_ref.at[pl.ds(h * HALF + q * QUART + s * SUB, SUB), cols]
            dst = a.at[p, pl.ds(h * QUART + s * SUB, SUB), place]
            snd, rcv = a2_snd.at[r, h, q, s], a2_sem.at[p, s]
            if r:
                copy = remote(src, dst, snd, rcv, dev(z, kk, y, h))
                pl.when(active)(copy.wait_send if sent else copy.start)
            else:
                copy = remote(src, dst, snd, rcv, sib)
                pl.when(active & (c != h))(copy.wait_send if sent else copy.start)
                if not sent:
                    local = pltpu.make_async_copy(src, dst, rcv)
                    pl.when(active & (c == h))(local.start)

    def a_piece(p, s, yy):
        return a.at[
            p,
            pl.ds(pl.multiple_of(c * QUART + s * SUB, SUB), SUB),
            pl.ds(pl.multiple_of(yy * ROWS, ROWS), ROWS),
        ]

    def a_half(p, yy, cc):
        return a.at[
            p,
            pl.ds(pl.multiple_of(cc * QUART, QUART), QUART),
            pl.ds(pl.multiple_of(yy * ROWS, ROWS), ROWS),
        ]

    def along(p, s, yy, snd, rcv, target):
        push(a_piece(p, s, yy), a_piece(p, s, yy), ay_snd.at[p, snd], rcv.at[p, s], target)

    def share(p, i, yy):
        push(a_half(p, yy, c), a_half(p, yy, c), sb_snd.at[p, i], sb_sem.at[p, i], sib)

    def a_own(p):
        arrived(a_piece(p, 0, y), a2_sem.at[p, 0])
        along(p, 0, y, 0, al_sem, yr)
        arrived(a_piece(p, 1, y), a2_sem.at[p, 1])
        along(p, 1, y, 1, ar_sem, yl)
        along(p, 1, y, 2, al_sem, yr)
        along(p, 0, y, 3, ar_sem, yl)
        share(p, 0, y)

    def a_relay(p):
        left, right = mod(y - 1), mod(y + 1)
        arrived(a_piece(p, 0, left), al_sem.at[p, 0])
        along(p, 0, left, 4, af_sem, yr)
        arrived(a_piece(p, 1, right), ar_sem.at[p, 1])
        along(p, 1, right, 5, af_sem, yl)

    def a_fwd(p):
        left, right = mod(y - 1), mod(y + 1)
        arrived(a_piece(p, 1, left), al_sem.at[p, 1])
        share(p, 1, left)
        arrived(a_piece(p, 0, right), ar_sem.at[p, 0])
        share(p, 2, right)

    def a_far(p):
        far = mod(y + 2)
        arrived(a_piece(p, 0, far), af_sem.at[p, 0])
        arrived(a_piece(p, 1, far), af_sem.at[p, 1])
        share(p, 3, far)

    def a_done(p):
        for i, yy in enumerate((y, mod(y - 1), mod(y + 1), mod(y + 2))):
            arrived(a_half(p, yy, 1 - c), sb_sem.at[p, i])

    def b_piece(j, s, zz):
        return b.at[j, pl.ds(pl.multiple_of(zz * ROWS + s * HALF, HALF), HALF), :]

    def b_send(j, s, right, sent=False):
        src = t_ref.at[pl.ds(s * HALF, HALF), pl.ds(j * JW, JW)]
        rcv = bl_sem.at[j, s] if right else br_sem.at[j, s]
        copy = remote(src, b_piece(j, s, z), b_snd.at[j, 2 * s + right], rcv, zr if right else zl)
        (copy.wait_send if sent else copy.start)()

    def b_own(j):
        for s, right in ((0, True), (1, False), (1, True), (0, False)):
            b_send(j, s, right)

    def b_right(j):
        left = mod(z - 1)
        arrived(b_piece(j, 0, left), bl_sem.at[j, 0])
        push(b_piece(j, 0, left), b_piece(j, 0, left), b_snd.at[j, 4], bf_sem.at[j, 0], zr)

    def b_left(j):
        right = mod(z + 1)
        arrived(b_piece(j, 1, right), br_sem.at[j, 1])
        push(b_piece(j, 1, right), b_piece(j, 1, right), b_snd.at[j, 5], bf_sem.at[j, 1], zl)

    def own_copy(j):
        rows = pl.ds(pl.multiple_of(z * ROWS, ROWS), ROWS)
        return pltpu.make_async_copy(t_ref.at[:, pl.ds(j * JW, JW)], b.at[j, rows, :], own_sem.at[j])

    def b_done(j):
        own_copy(j).wait()
        arrived(b_piece(j, 1, mod(z - 1)), bl_sem.at[j, 1])
        arrived(b_piece(j, 0, mod(z + 1)), br_sem.at[j, 0])
        for s in range(2):
            arrived(b_piece(j, s, mod(z + 2)), bf_sem.at[j, s])

    def block(ref, q, h, j):
        return ref.at[j, pl.ds(q * HALF + h * QUART, QUART), :]

    def unit(s0, s1, s2, out, p, first, count):
        kind, q = p // 2, p % 2
        rows = pl.ds(q * HALF, HALF)
        source = (s0, s1, s2, None)[kind]

        def step(j):
            cols = pl.ds(j * JW if count == 1 else pl.multiple_of(j * JW, JW), JW)
            if kind == 1:
                for h in range(2):
                    arrived(block(rf, q, h, j), rf_sem.at[q, h, j])
            acc = jnp.dot(a[p], b[j], preferred_element_type=jnp.float32)
            if kind == 1:
                acc = acc + rf[j, rows, :].astype(jnp.float32)
            if kind == 3:
                for h in range(2):
                    out[pl.ds(h * HALF + q * QUART, QUART), cols] = acc[h * QUART : (h + 1) * QUART]
                return
            source[j, rows, :] = acc.astype(jnp.bfloat16)
            for h in range(2):
                reduce_copy(source, p, h, j).start()

        if count == 1:
            step(first)
        else:
            lax.fori_loop(first, first + count, lambda j, carry: (step(j), carry)[1], 0)

    def reduce_copy(source, p, h, j):
        kind, q = p // 2, p % 2
        target = xr if (h == 0) == (kind < 2) else xl
        into, sem = (rf, rf_sem) if kind == 0 else (rp, rp_sem) if target is xr else (rm, rm_sem)
        return remote(
            block(source, q, h, j), block(into, q, h, j), x_snd.at[p, h, j], sem.at[q, h, j], target
        )

    def final(out, q, j):
        cols = pl.ds(j * JW, JW)
        rows = pl.ds(q * HALF, HALF)
        for h in range(2):
            arrived(block(rp, q, h, j), rp_sem.at[q, h, j])
            arrived(block(rm, q, h, j), rm_sem.at[q, h, j])
        for h in range(2):
            rows = pl.ds(q * HALF + h * QUART, QUART)
            into = pl.ds(h * HALF + q * QUART, QUART)
            out[into, cols] = (
                out[into, cols] + rp[j, rows, :].astype(jnp.float32) + rm[j, rows, :].astype(jnp.float32)
            )

    def build(edge_ref, padded, emb, wide, sel, w, base, direct, mirror):
        w_copy = pltpu.make_async_copy(w_hbm, w, w_sem)
        base_copy = pltpu.make_async_copy(base_hbm, base, base_sem)
        w_copy.start()
        base_copy.start()

        barrier = pltpu.get_barrier_semaphore()
        for d in ROW_ORDER:
            pl.semaphore_signal(
                barrier, inc=1, device_id=((row + d) % 16, col), device_id_type=MESH
            )
        for d in range(1, 4):
            pl.semaphore_signal(
                barrier, inc=1, device_id=dev(z, mod(x + d), y, 1 - c), device_id_type=MESH
            )
        for d in COL_ORDER:
            pl.semaphore_signal(
                barrier, inc=1, device_id=(row, (col + d) % 8), device_id_type=MESH
            )
        padded[...] = jnp.zeros((8, ORB), jnp.float32)
        padded[0:3, 0:8] = vec_ref[...]
        padded[3:5, 0:8] = atoms_ref[...].astype(jnp.float32)
        packed = padded[0:1, :]
        for n in range(1, 5):
            packed = packed + pltpu.roll(padded[n : n + 1, :], 8 * n, 1)
        edge_ref[...] = packed
        pl.semaphore_wait(barrier, 25)

        mine = row * 8 + col
        own = pltpu.make_async_copy(edge_ref, edges.at[pl.ds(mine, 1), :], edge_sem)
        own.start()
        copies = []
        for d in COL_ORDER:
            copy = pltpu.make_async_remote_copy(
                src_ref=edge_ref, dst_ref=edges.at[pl.ds(mine, 1), :],
                send_sem=snd.at[d], recv_sem=rcv.at[d],
                device_id=(row, (col + d) % 8), device_id_type=MESH,
            )
            copy.start()
            copies.append(copy)
        own.wait()
        for d in COL_ORDER:
            src = row * 8 + (col + 8 - d) % 8
            pltpu.make_async_remote_copy(
                src_ref=edge_ref, dst_ref=edges.at[pl.ds(src, 1), :],
                send_sem=snd.at[d], recv_sem=rcv.at[d],
                device_id=(row, (col + d) % 8), device_id_type=MESH,
            ).wait_recv()

        def group(r):
            return edges.at[pl.ds(pl.multiple_of(r * 8, 8), 8), :]

        for d in ROW_ORDER:
            copy = pltpu.make_async_remote_copy(
                src_ref=group(row), dst_ref=group(row),
                send_sem=snd.at[7 + d], recv_sem=rcv.at[7 + d],
                device_id=((row + d) % 16, col), device_id_type=MESH,
            )
            copy.start()
            copies.append(copy)
        for d in ROW_ORDER:
            src = (row + 16 - d) % 16
            pltpu.make_async_remote_copy(
                src_ref=group(src), dst_ref=group(src),
                send_sem=snd.at[7 + d], recv_sem=rcv.at[7 + d],
                device_id=((row + d) % 16, col), device_id_type=MESH,
            ).wait_recv()

        fields = edges[...].T
        vx, vy, vz = fields[0:8], fields[8:16], fields[16:24]
        first, second = fields[24:32], fields[32:40]
        radius = jnp.sqrt(vx * vx + vy * vy + vz * vz + 0.25)
        ux, uy, uz = vx / radius, vy / radius, vz / radius
        harmonics = [
            None, ux, uy, uz, ux * uy, uy * uz, uz * ux, ux * ux - uy * uy, 3.0 * uz * uz - 1.0
        ]
        for k in range(NR):
            scaled = (radius - (1.0 + 0.3 * k)) / 0.5
            radial = jnp.exp(-(scaled * scaled))
            for m in range(9):
                f = 9 * k + m
                emb[f * 8 : f * 8 + 8, :] = radial if m == 0 else radial * harmonics[m]
        number = lax.broadcasted_iota(jnp.int32, (PADDED, ORB), 0)
        upper_atom = jnp.zeros((PADDED, ORB), jnp.int32)
        for n in range(1, RB):
            upper_atom = upper_atom + jnp.where(number >= CB * n, 1, 0)
        pair = (row * RB + upper_atom) * NB + col * CB + number - CB * upper_atom
        pair = pair.astype(jnp.float32)
        forward = first * float(NB) + second
        backward = second * float(NB) + first
        for i in range(8):
            lanes = slice(i * ORB, (i + 1) * ORB)
            for h in range(2):
                wanted = pair + float(h * RB // 2 * NB)
                at = 2 * PADDED * h
                sel[at : at + PADDED, lanes] = jnp.where(forward[i : i + 1] == wanted, 1.0, 0.0)
                sel[at + PADDED : at + 2 * PADDED, lanes] = jnp.where(
                    backward[i : i + 1] == wanted, 1.0, 0.0
                )
            wide[:, lanes] = emb[pl.ds(i, FEAT, stride=8), :]
        coefficient = lax.dot_general(
            sel[...], wide[...], (((1,), (1,)), ((), ())),
            precision=lax.Precision.HIGHEST, preferred_element_type=jnp.float32,
        ).astype(jnp.bfloat16)

        for copy in copies:
            copy.wait_send()
        w_copy.wait()

        base_copy.wait()
        upper = upper_ref[0]
        scale = upper - lower_ref[0]
        on_diagonal = lax.broadcasted_iota(jnp.int32, (ORB, ORB), 0) == lax.broadcasted_iota(
            jnp.int32, (ORB, ORB), 1
        )

        def expand(n, carry):
            start = pl.multiple_of(n * 8 * ORB, 8 * ORB)
            part = jnp.dot(
                coefficient, w[:, pl.ds(start, 8 * ORB)], preferred_element_type=jnp.float32
            )
            place = pl.ds(pl.multiple_of(n * 8, 8), 8)
            for h in range(2):
                at = 2 * PADDED * h
                direct[h, :, place, :] = part[at : at + PADDED].reshape(PADDED, 8, ORB)
                at = at + PADDED
                mirror[h, :, place, :] = part[at : at + PADDED].reshape(PADDED, 8, ORB)
            return carry

        lax.fori_loop(0, ORB // 8, expand, 0)
        inverse = 1.0 / scale

        def half_tile(h):
            def finish(i, carry):
                rows = pl.ds(pl.multiple_of(h * HALF + i * ORB, ORB), ORB)
                for k in range(CB):
                    lanes = slice(k * ORB, (k + 1) * ORB)
                    both = direct[h, i * CB + k] + mirror[h, i * CB + k].T
                    both = both + base[rows, lanes].astype(jnp.float32)
                    atom = row * RB + h * (RB // 2) + i
                    shift = jnp.where(atom == col * CB + k, upper, 0.0)
                    moved = jnp.where(on_diagonal, shift, 0.0) - both
                    t_ref[rows, lanes] = (moved * inverse).astype(jnp.bfloat16)
                return carry

            lax.fori_loop(0, RB // 2, finish, 0)

        half_tile(0)
        for r, h, q in ((3, 0, 0), (3, 0, 1), (2, 0, 0)):
            exchange(r, h, q)
        b_send(0, 0, True)
        b_send(0, 0, False)
        for q in range(2):
            exchange(0, 0, q)
        half_tile(1)
        for r, h, q in (
            (1, 1, 0), (1, 1, 1), (2, 1, 0), (2, 0, 1), (2, 1, 1),
            (1, 0, 0), (3, 1, 0), (1, 0, 1), (3, 1, 1),
        ):
            exchange(r, h, q)
        b_send(0, 1, True)
        b_send(0, 1, False)
        for q in range(2):
            exchange(0, 1, q)

    f32 = jnp.float32
    pl.run_scoped(
        build,
        pltpu.VMEM((1, ORB), f32),
        pltpu.VMEM((8, ORB), f32),
        pltpu.VMEM((FEAT * 8, ORB), f32),
        pltpu.VMEM((FEAT, EDGES), f32),
        pltpu.VMEM((4 * PADDED, EDGES), f32),
        pltpu.VMEM((FEAT, ORB * ORB), jnp.bfloat16),
        pltpu.VMEM((ROWS, COLS), jnp.bfloat16),
        pltpu.VMEM((2, PADDED, ORB, ORB), f32),
        pltpu.VMEM((2, PADDED, ORB, ORB), f32),
    )

    def work(s0, s1, s2):
        out = o_ref
        for j in range(NJ):
            own_copy(j).start()
        steps = {
            "a_own": a_own, "a_relay": a_relay, "a_fwd": a_fwd, "a_far": a_far, "a_done": a_done,
            "b_own": b_own, "b_right": b_right, "b_left": b_left, "b_done": b_done,
        }
        for name, *args in plan()[0]:
            if name == "unit":
                unit(s0, s1, s2, out, *args)
            elif name == "final":
                final(out, *args)
            else:
                steps[name](*args)
        for copy in pending:
            copy.wait_send()
        for i in range(16):
            exchange(i // 4, i // 2 % 2, i % 2, True)
        for i in range(4 * NJ):
            b_send(i // 4, i // 2 % 2, i % 2 == 0, True)
        for p in range(6):
            for h in range(2):
                for j in range(NJ):
                    reduce_copy((s0, s1, s2)[p // 2], p, h, j).wait_send()

    tiles = pltpu.VMEM((NJ, ROWS, JW), jnp.bfloat16)
    pl.run_scoped(work, tiles, tiles, tiles)


def square(vec, atoms, lower, upper, weight, base):
    dma = pltpu.SemaphoreType.DMA
    bf = jnp.bfloat16
    return pl.pallas_call(
        square_kernel,
        out_shape=pltpu.VMEM((ROWS, COLS), jnp.float32),
        in_specs=[
            pl.BlockSpec(memory_space=pltpu.VMEM),
            pl.BlockSpec(memory_space=pltpu.VMEM),
            pl.BlockSpec(memory_space=pltpu.SMEM),
            pl.BlockSpec(memory_space=pltpu.SMEM),
            pl.BlockSpec(memory_space=pl.ANY),
            pl.BlockSpec(memory_space=pl.ANY),
        ],
        out_specs=pl.BlockSpec(memory_space=pltpu.VMEM),
        scratch_shapes=[
            pltpu.VMEM((ORB, ORB), jnp.float32),
            pltpu.VMEM((ROWS, COLS), bf),
            pltpu.VMEM((8, HALF, K), bf),
            pltpu.VMEM((NJ, K, JW), bf),
            pltpu.VMEM((NJ, ROWS, JW), bf),
            pltpu.VMEM((NJ, ROWS, JW), bf),
            pltpu.VMEM((NJ, ROWS, JW), bf),
            dma, dma, dma, dma((23,)), dma((23,)),
            dma((8, 2)), dma((8, 2)), dma((8, 2)), dma((8, 2)), dma((8, 4)),
            dma((NJ, 2)), dma((NJ, 2)), dma((NJ, 2)),
            dma((2, 2, NJ)), dma((2, 2, NJ)), dma((2, 2, NJ)),
            dma((4, 2, 2, 2)), dma((8, 6)), dma((8, 4)), dma((NJ, 6)), dma((6, 2, NJ)),
            dma((NJ + 1,)),
        ],
        compiler_params=pltpu.CompilerParams(
            collective_id=0, has_side_effects=True, vmem_limit_bytes=56 * 2**20
        ),
        name="square",
    )(vec, atoms, lower, upper, weight, base)


def shards(edge_vec, edge_atoms, block_weight, base_hamiltonian, lower_bound, upper_bound):
    return square(
        edge_vec, edge_atoms, lower_bound, upper_bound, block_weight, base_hamiltonian
    )


def solution(mesh):
    return jax.shard_map(
        shards,
        mesh=mesh,
        in_specs=(P(None, ("row", "col")), P(None, ("row", "col")), P(), P("row", "col"), P(), P()),
        out_specs=P("row", "col"),
        check_vma=False,
    )
```
